32 devices in a mesh: blk: 8 (over z, y), lon: 4 (over x, core).
Axes of the slice: x: 2, y: 2, z: 4, core: 2. Of those that a mesh axis runs over, the one named last changes fastest.
Arguments:
- anomalies: float32 [16, 1152, 4320], P(None, 'blk', 'lon'), may hold values from -6 to 6
- classes: int32 [1152, 4320], P('blk', 'lon'), may hold values from 0 to 3
- legendre: float32 [32, 2160, 1152], P('blk', 'lon'), may hold values from -0.0234375 to 0.0234375
- precond: float32 [32, 16, 135, 135], P('blk', 'lon'), may hold values from -1 to 2, as said below
- prior: float32 [2160], P('lon'), may hold values from 0.05 to 0.5
- assign: int32 [32], replicated, may hold values from 0 to 31, as said below
Outputs:
- solution: float32 [32, 2, 16, 2160], P('blk', None, None, 'lon')
- residual: float32 [32, 2, 16, 2160], P('blk', None, None, 'lon')
The draws below stay inside these ranges and needn't reach their ends.
Inputs may be any that keep to these rules, and one draw needn't show every extreme that they name: `assign`: A permutation of the order indices; the 4 slots of each index of blk hold 2 pairs q and 31 - q. `precond`: each block is symmetric, and its diagonal entries exceed the sum of the magnitudes of the other entries of their row.
All inputs are finite; a program needn't handle non-finite values.
Results may differ from the reference program's by a relative error of at most 0.00026.
Values sent between devices are 32-bit elements; how exact they have to be, the bound alone decides.
A program may use at most 128 MiB of HBM per device.

```python
import math
import jax
import jax.numpy as jnp
from jax import lax

L = 2160
NLON = 4320
NR = 1152
BLOCK = 135
ITERS = 2
NRHS = 16
M_WIN = 32
STRIDE = 67
NB = 16


def draw_precond(key, part):
    key_off = jax.random.fold_in(key, 11)
    key_diag = jax.random.fold_in(key, 12)
    raw_values = jax.random.uniform(key_off, (M_WIN, NB, BLOCK, BLOCK), jnp.float32, -1.0, 1.0) / BLOCK
    symmetric = 0.5 * (raw_values + jnp.swapaxes(raw_values, 2, 3))
    diagonal = jax.random.uniform(key_diag, (M_WIN, NB, BLOCK), jnp.float32, 1.0, 2.0)
    identity = jnp.eye(BLOCK, dtype=jnp.float32)
    return symmetric * (1.0 - identity) + diagonal[..., None] * identity


def draw_assign(key, part):
    half_count = M_WIN // 2
    shuffled = jax.random.permutation(jax.random.fold_in(key, 21), half_count)
    flip_bits = jax.random.randint(jax.random.fold_in(key, 22), (half_count,), 0, 2)
    first_slot = jnp.where(flip_bits == 1, M_WIN - 1 - shuffled, shuffled)
    second_slot = M_WIN - 1 - first_slot
    return jnp.stack([first_slot, second_slot], axis=1).reshape(M_WIN).astype(jnp.int32)


def set_ends(result, stream_key, low, top_value):
    shape = result.shape
    spot = [jax.random.randint(jax.random.fold_in(stream_key, axis), (), 0, shape[axis]) for axis in range(len(shape))]
    result = result.at[tuple(spot)].set(low)
    longest = shape.index(max(shape))
    spot[longest] = (spot[longest] + 1) % shape[longest]
    return result.at[tuple(spot)].set(top_value)


def block_scale(key, extent, shards, smallest, top_value):
    level, own = 1.0, jax.random.fold_in(key, 6)
    for axis_at, shards_of in shards:
        draws = jnp.exp(jax.random.uniform(jax.random.fold_in(own, axis_at), (shards_of,), jnp.float32, smallest / len(shards), top_value / len(shards)))
        level = level * jnp.repeat(draws, extent[axis_at] // shards_of).reshape([-1 if axis == axis_at else 1 for axis in range(len(extent))])
    return level


def centred(rng, dims, scale, limit, split=(), held_as=jnp.bfloat16):
    array = scale * jax.random.normal(rng, dims, jnp.float32)
    if split:
        array = array * block_scale(rng, dims, split, -0.22, 0.18)
    return jnp.clip(array, -limit, limit).astype(held_as)


def setup_inputs(seed: int = 0) -> dict:
    key_list = jax.random.split(jax.random.key(seed), 7)
    anomalies = centred(key_list[0], (NRHS, NR, NLON), 1.0, 6.0, ((1, 8), (2, 4)), jnp.float32)
    classes = set_ends(jax.random.randint(key_list[1], (NR, NLON), 0, 4), jax.random.fold_in(key_list[1], 1), 0, 3).astype(jnp.int32)
    legendre = centred(key_list[2], (M_WIN, L, NR), (L * M_WIN) ** -0.5, 0.0234375, ((0, 8), (1, 4)), jnp.float32)
    precond = draw_precond(jax.random.fold_in(key_list[6], 71), 0)
    prior = jnp.clip(jnp.exp(math.log(0.5) - 2.3025851 * jax.random.uniform(key_list[4], (L,), jnp.float32) ** block_scale(key_list[4], (L,), ((0, 4),), -0.2, 0.2)), 0.05, 0.5)
    assign = draw_assign(jax.random.fold_in(key_list[6], 71), 0)
    return {"anomalies": anomalies, "classes": classes, "legendre": legendre, "precond": precond, "prior": prior, "assign": assign}


HUBER_LEVELS = (1.0, 0.5, 0.25, 0.125)
HIGHEST = lax.Precision.HIGHEST


def build_mask(orders, first_degree, degrees):
    degree = first_degree + jnp.arange(degrees, dtype=jnp.int32)
    upper_part = (degree[None, :] >= orders[:, None]).astype(jnp.float32)
    sine_keep = upper_part * (orders[:, None] > 0).astype(jnp.float32)
    return jnp.stack([upper_part, sine_keep], axis=1)[:, :, None, :]


def trig_table(orders, first_col, columns, lon_total):
    column = first_col + jnp.arange(columns, dtype=jnp.int32)
    phases = (orders[:, None] * column[None, :]) % lon_total
    angles = phases.astype(jnp.float32) * (2.0 * math.pi / lon_total)
    return jnp.stack([jnp.cos(angles), jnp.sin(angles)], axis=1)


def huber_weights(classes):
    weighted = jnp.zeros(classes.shape, jnp.float32)
    for level_index in range(4):
        weighted = weighted + (classes == level_index).astype(jnp.float32) * HUBER_LEVELS[level_index]
    return weighted


def reference(anomalies, classes, legendre, precond, prior, assign):
    orders = (assign * STRIDE).astype(jnp.int32)
    live_mask = build_mask(orders, 0, L)
    trig_rows = trig_table(orders, 0, NLON, NLON)
    weights = huber_weights(classes)

    def forward(coeffs):
        cycles_part = jnp.einsum("scnl,slr->scnr", coeffs, legendre, precision=HIGHEST)
        return jnp.einsum("scnr,sck->nrk", cycles_part, trig_rows, precision=HIGHEST)

    def adjoint(grid_field):
        cycles_part = jnp.einsum("nrk,sck->scnr", grid_field, trig_rows, precision=HIGHEST)
        return jnp.einsum("scnr,slr->scnl", cycles_part, legendre, precision=HIGHEST)

    def normal(coeffs):
        return live_mask * (adjoint(weights[None] * forward(coeffs)) + prior * coeffs)

    def precondition(coeffs):
        blocks = coeffs.reshape(M_WIN, 2, NRHS, NB, BLOCK)
        applied = jnp.einsum("sbij,scnbj->scnbi", precond, blocks, precision=HIGHEST)
        return live_mask * applied.reshape(coeffs.shape)

    def column_dot(lhs_values, rhs_values):
        return jnp.sum(lhs_values * rhs_values, axis=(0, 1, 3))

    def spread(values):
        return values[None, None, :, None]

    residual = live_mask * adjoint(weights[None] * anomalies)
    solution = jnp.zeros_like(residual)
    search = precondition(residual)
    fit_now = column_dot(residual, search)
    direction = search
    for iteration in range(ITERS):
        image_vec = normal(direction)
        alpha_step = fit_now / column_dot(direction, image_vec)
        solution = solution + spread(alpha_step) * direction
        residual = residual - spread(alpha_step) * image_vec
        if iteration + 1 < ITERS:
            search = precondition(residual)
            fit_next = column_dot(residual, search)
            direction = search + spread(fit_next / fit_now) * direction
            fit_now = fit_next
    return solution, residual
```

```python
import functools
import math

import jax
import jax.numpy as jnp
from jax import lax
from jax.experimental import pallas as pl
from jax.experimental.pallas import tpu as pltpu
from jax.sharding import PartitionSpec as P

ITERS = 2


HUBER_LEVELS = (1.0, 0.5, 0.25, 0.125)
HIGHEST = lax.Precision.HIGHEST
GROUP = 8
MESH = pl.DeviceIdType.MESH
VMEM_WHOLE = pl.BlockSpec(memory_space=pltpu.VMEM)


def build_mask(orders, first_degree, degrees):
    degree = first_degree + jnp.arange(degrees, dtype=jnp.int32)
    upper_part = (degree[None, :] >= orders[:, None]).astype(jnp.float32)
    sine_keep = upper_part * (orders[:, None] > 0).astype(jnp.float32)
    return jnp.stack([upper_part, sine_keep], axis=1)[:, :, None, :]


def trig_table(orders, first_col, columns, lon_total):
    column = first_col + jnp.arange(columns, dtype=jnp.int32)
    phases = orders[:, None] * column[None, :] % lon_total
    angles = phases.astype(jnp.float32) * (2.0 * math.pi / lon_total)
    return jnp.stack([jnp.cos(angles), jnp.sin(angles)], axis=1)


def huber_weights(classes):
    weighted = jnp.zeros(classes.shape, jnp.float32)
    for level_index in range(4):
        weighted = (
            weighted + (classes == level_index).astype(jnp.float32) * HUBER_LEVELS[level_index]
        )
    return weighted


def legendre_up(coeffs, basis_rows):
    return jnp.einsum("scnl,slr->scnr", coeffs, basis_rows, precision=HIGHEST)


def legendre_down(cycles_part, basis_rows):
    return jnp.einsum("scnr,slr->scnl", cycles_part, basis_rows, precision=HIGHEST)


def plain_body(anomalies, classes, legendre, precond, prior, assign):
    lon_count = lax.axis_size("lon")
    blk_count = lax.axis_size("blk")
    blk_place = lax.axis_index("blk")
    lon_place = lax.axis_index("lon")
    slot_count = legendre.shape[0]
    local_degrees = legendre.shape[1]
    rhs_count = anomalies.shape[0]
    cycle_count = anomalies.shape[1]
    longitudes = anomalies.shape[2]
    window = assign.shape[0]
    block_width = precond.shape[2]
    quarter = slot_count // lon_count
    grid_rows = rhs_count * cycle_count
    stride_value = local_degrees * lon_count // window
    all_orders = assign * stride_value
    own_orders = lax.dynamic_slice_in_dim(all_orders, blk_place * slot_count, slot_count)
    first_degree = lon_place * local_degrees
    first_column = lon_place * longitudes
    live_mask = build_mask(own_orders, first_degree, local_degrees)
    weights = huber_weights(classes)
    row_orders = (
        all_orders.reshape(blk_count, lon_count, quarter).transpose(1, 0, 2).reshape(window)
    )
    trig_rows = trig_table(row_orders, first_column, longitudes, longitudes * lon_count).reshape(
        2 * window, longitudes
    )

    def analyse(grid_field):
        flat_grid = grid_field.reshape(grid_rows, longitudes)
        product = lax.dot_general(trig_rows, flat_grid, (((1,), (1,)), ((), ())), precision=HIGHEST)
        shared = lax.psum_scatter(
            product.reshape(window // lon_count * lax.axis_size("lon"), 2, rhs_count, cycle_count),
            "lon",
            scatter_dimension=0,
            tiled=True,
        )
        returned = lax.all_to_all(shared, "blk", split_axis=0, concat_axis=3, tiled=True)
        return legendre_down(lax.all_gather(returned, "lon", axis=0, tiled=True), legendre)

    def precondition(coeffs):
        blocks = coeffs.reshape(slot_count, 2, rhs_count, local_degrees // block_width, block_width)
        applied = jnp.einsum("sbij,scnbj->scnbi", precond, blocks, precision=HIGHEST)
        return live_mask * applied.reshape(coeffs.shape)

    def column_dot(lhs_values, rhs_values):
        return jnp.sum(lhs_values * rhs_values, axis=(0, 1, 3))

    def spread(values):
        return values[None, None, :, None]

    def fit_sum(lhs_values, rhs_values):
        return lax.psum(column_dot(lhs_values, rhs_values), ("blk", "lon"))

    residual = live_mask * analyse(weights * anomalies)
    solution = jnp.zeros_like(residual)
    search = precondition(residual)
    fit_now = fit_sum(residual, search)
    direction = search
    for iteration in range(ITERS):
        synthesize_coeffs = direction
        synthesize_shared = lax.psum_scatter(
            legendre_up(synthesize_coeffs, legendre), "lon", scatter_dimension=0, tiled=True
        )
        moved = lax.all_to_all(synthesize_shared, "blk", split_axis=3, concat_axis=0, tiled=True)
        flat_orders = lax.all_gather(moved, "lon", axis=0, tiled=True).reshape(-1, grid_rows)
        grid_flat = lax.dot_general(
            flat_orders, trig_rows, (((0,), (0,)), ((), ())), precision=HIGHEST
        )
        image_vec = live_mask * (
            analyse(weights * grid_flat.reshape(rhs_count, cycle_count, longitudes))
            + prior * direction
        )
        curvature_sum = lax.psum(column_dot(direction, image_vec), ("blk", "lon"))
        alpha_step = fit_now / curvature_sum
        solution = solution + spread(alpha_step) * direction
        residual = residual - spread(alpha_step) * image_vec
        if iteration + 1 < ITERS:
            search = precondition(residual)
            fit_next = fit_sum(residual, search)
            direction = search + spread(fit_next / fit_now) * direction
            fit_now = fit_next
    return (solution, residual)


def split(values):
    high = values.astype(jnp.bfloat16)
    return high, (values - high.astype(jnp.float32)).astype(jnp.bfloat16)


def split_outside(values):
    high = lax.reduce_precision(values, 8, 7)
    return high.astype(jnp.bfloat16), (values - high).astype(jnp.bfloat16)


def exchange_kernel(
    blocks, p_ref, o_ref, from_core, summed, from_x, ready, send_sem, recv_sem
):
    blk = lax.axis_index("blk")
    lon = lax.axis_index("lon")
    core, x = lon % 2, lon // 2
    core_mate = (blk, lon + 1 - 2 * core)
    x_mate = (blk, lon + 2 - 4 * x)
    part = from_x.shape[1]
    mine = pl.ds(pl.multiple_of(part * x, 8), part)
    theirs = pl.ds(pl.multiple_of(part * (1 - x), 8), part)
    barrier = pltpu.get_barrier_semaphore()
    peers = [core_mate, x_mate] + [((blk + j) % blocks, lon) for j in range(1, blocks)]
    for peer in peers:
        pl.semaphore_signal(barrier, inc=1, device_id=peer, device_id_type=MESH)
    pl.semaphore_wait(barrier, len(peers))

    def copy(stage, j, src, dst, peer):
        return pltpu.make_async_remote_copy(
            src_ref=src,
            dst_ref=dst,
            send_sem=send_sem.at[stage, j],
            recv_sem=recv_sem.at[stage, j],
            device_id=peer,
            device_id_type=MESH,
        )

    order = sorted(range(blocks), key=lambda j: (j == 0, abs(j - blocks // 2)))
    started = {}

    def launch(stage, j, src, dst, peer):
        started[stage, j] = copy(stage, j, src, dst, peer)
        started[stage, j].start()

    for j in order:
        to = (blk + j) % blocks
        launch(0, j, p_ref.at[to, 1 - core], from_core.at[to], core_mate)

    def over_x(j):
        to = (blk + j) % blocks
        started[0, j].wait_recv()
        summed[to] = p_ref[to, core] + from_core[to]
        launch(1, j, summed.at[to, theirs], from_x.at[to], x_mate)

    def over_blk(j):
        to = (blk + j) % blocks
        started[1, j].wait_recv()
        value = summed[to, mine] + from_x[to]
        if j == 0:
            o_ref[blk, core, mine] = value
        else:
            ready[to] = value
            launch(2, j, ready.at[to], o_ref.at[blk, core, mine], (to, lon))

    for step in range(blocks + 2):
        if step < blocks:
            over_x(order[step])
        if step >= 2:
            over_blk(order[step - 2])
    arrivals = order[-1:] + order[:-1]
    for j in arrivals:
        source = (blk - j + blocks) % blocks
        if j:
            started[2, j].wait_recv()
        held = o_ref.at[source, core, mine]
        launch(3, j, held, held, x_mate)
        launch(4, j, held, held, core_mate)
    for j in arrivals:
        source = (blk - j + blocks) % blocks
        started[3, j].wait_recv()
        held = o_ref.at[source, core, theirs]
        launch(5, j, held, held, core_mate)
    for j in arrivals:
        started[4, j].wait_recv()
        started[5, j].wait_recv()
    for one in started.values():
        one.wait_send()


def exchange(partial):
    blocks, halves, padded, lanes = partial.shape
    return pl.pallas_call(
        functools.partial(exchange_kernel, blocks),
        out_shape=jax.ShapeDtypeStruct(partial.shape, jnp.float32),
        in_specs=[VMEM_WHOLE],
        out_specs=VMEM_WHOLE,
        scratch_shapes=[
            pltpu.VMEM((blocks, padded, lanes), jnp.float32),
            pltpu.VMEM((blocks, padded, lanes), jnp.float32),
            pltpu.VMEM((blocks, padded // 2, lanes), jnp.float32),
            pltpu.VMEM((blocks, padded // 2, lanes), jnp.float32),
            pltpu.SemaphoreType.DMA((6, blocks)),
            pltpu.SemaphoreType.DMA((6, blocks)),
        ],
        compiler_params=pltpu.CompilerParams(collective_id=0, has_side_effects=True),
        name="exchange",
    )(partial)


def group_sum(tile, group):
    lanes = tile.shape[1]
    at = lax.broadcasted_iota(jnp.int32, tile.shape, 1)
    shift = 1
    while shift < group:
        ahead = pltpu.roll(tile, lanes - shift, 1)
        behind = pltpu.roll(tile, shift, 1)
        tile = tile + jnp.where(at // shift % 2 == 0, ahead, behind)
        shift *= 2
    return tile


def sums_of(o_ref, half, group):
    tile = o_ref[0, 0, half:half + 8]
    for b in range(1, o_ref.shape[0]):
        tile = tile + o_ref[b, 0, half:half + 8]
    return group_sum(tile, group)


def pick_row(tile, row):
    return tile[row:row + 1]


def tile_of(rows):
    lanes = rows[0].shape[1]
    at = lax.broadcasted_iota(jnp.int32, (8, lanes), 0)
    tile = jnp.zeros((8, lanes), jnp.float32)
    for index, row in enumerate(rows):
        tile = jnp.where(at == index, jnp.broadcast_to(row, (8, lanes)), tile)
    return tile


def grid_kernel(kind, half, *refs):
    columns = pl.num_programs(0)
    n = pl.program_id(0)
    if kind == "data":
        field, weights, trig_down, trig_low, p_ref, down = refs
    elif kind == "first":
        o_ref, weights, trig_up, trig_down, trig_low, p_ref, q_ref, down, up, cycles = refs
    else:
        (o_ref, old_ref, old_q, weights, trig_up, trig_down, trig_low,
         p_ref, q_ref, down, up, cycles) = refs
    blocks, lanes = down.shape[0], down.shape[1]
    group = GROUP
    if kind != "data":
        @pl.when(n == 0)
        def _():
            sums = sums_of(o_ref, half, group)
            if kind == "first":
                q_ref[...] = sums
            else:
                before = old_q[...]
                beta = pick_row(sums, 0) / pick_row(before, 0)
                norm = (
                    pick_row(sums, 1)
                    + 2.0 * beta * pick_row(sums, 2)
                    + beta * beta * pick_row(before, 1)
                )
                q_ref[...] = tile_of([pick_row(sums, 0), norm, beta])
            for b in range(blocks):
                for h in range(2):
                    rows = o_ref[b, h, 0:half]
                    if kind != "first":
                        rows = rows + beta * old_ref[b, h, 0:half]
                    cycles[b, h * half:(h + 1) * half] = rows
                up[b] = cycles[b].T

        stack = jnp.concatenate(
            [up[b, pl.ds(pl.multiple_of(n * group, 8), group), :] for b in range(blocks)], axis=0
        )
        high = stack.astype(jnp.bfloat16).astype(jnp.float32)
        triple = jnp.concatenate([high, high, stack - high], axis=0).T.astype(jnp.bfloat16)
        grid_field = jnp.dot(triple, trig_up[...], preferred_element_type=jnp.float32)
    else:
        grid_field = field[0]
    high, low = split(grid_field * weights[...])
    sums = jnp.dot(high, trig_down[...], preferred_element_type=jnp.float32)
    sums = sums + jnp.dot(low, trig_low[...], preferred_element_type=jnp.float32)
    sums = sums.T
    sums = sums[: 8 * blocks] + sums[8 * blocks:]
    for b in range(blocks):
        down[b, pl.ds(pl.multiple_of(n * group, 8), group), :] = sums[8 * b:8 * b + 8]

    @pl.when(n == columns - 1)
    def _():
        total = jnp.zeros((1, lanes), jnp.float32)
        for b in range(blocks):
            rows = down[b].T
            if kind != "data":
                total = total + jnp.sum(rows * cycles[b], axis=0, keepdims=True)
            for h in range(2):
                p_ref[b, h, 0:half] = rows[h * half:(h + 1) * half]
        for b in range(blocks):
            for h in range(2):
                p_ref[b, h, half:] = jnp.zeros((p_ref.shape[2] - half, lanes), jnp.float32)
            if kind != "data":
                p_ref[b, 0, half:half + 8] = tile_of([total])


def grid_call(kind, blocks, lanes, cycle_count, rhs_count, *operands):
    half = cycle_count // 2
    padded = -(-(half + 8) // 16) * 16
    out_shape = [jax.ShapeDtypeStruct((blocks, 2, padded, lanes), jnp.float32)]
    scratch = [pltpu.VMEM((blocks, lanes, cycle_count), jnp.float32)]
    in_specs = [VMEM_WHOLE] * len(operands)
    if kind == "data":
        in_specs[0] = pl.BlockSpec((1,) + operands[0].shape[1:], lambda n: (n, 0, 0))
    else:
        out_shape.append(jax.ShapeDtypeStruct((8, lanes), jnp.float32))
        scratch.append(pltpu.VMEM((blocks, lanes, cycle_count), jnp.float32))
        scratch.append(pltpu.VMEM((blocks, cycle_count, lanes), jnp.float32))
    return pl.pallas_call(
        functools.partial(grid_kernel, kind, half),
        grid=(rhs_count,),
        out_shape=out_shape,
        in_specs=in_specs,
        out_specs=[VMEM_WHOLE] * len(out_shape),
        scratch_shapes=scratch,
        compiler_params=pltpu.CompilerParams(vmem_limit_bytes=60 << 20),
        name="grid_" + kind,
    )(*operands)


def to_column(row):
    return jnp.broadcast_to(row, (row.shape[1], row.shape[1])).T


def product(lhs, high, low, dims):
    lhs_high, lhs_low = split(lhs)
    rows = lhs.shape[0]
    both = jnp.concatenate([lhs_high, lhs_low], axis=0)
    first = lax.dot_general(both, high, dims, preferred_element_type=jnp.float32)
    second = lax.dot_general(lhs_high, low, dims, preferred_element_type=jnp.float32)
    return first[:rows] + first[rows:] + second


NN = (((1,), (0,)), ((), ()))
NT = (((1,), (1,)), ((), ()))


def coeff_kernel(kind, half, *refs):
    s = pl.program_id(0)
    if kind == "first":
        (o_ref, leg_high, leg_low, pre_high, pre_low, live, prior,
         p_ref, residual, z_out, spread_down, turned_down, tiles, up, dots) = refs
    elif kind == "middle":
        (o_ref, q_ref, leg_high, leg_low, pre_high, pre_low, live, prior, old, direction,
         p_ref, residual, z_out, solution, spread_down, turned_down, tiles, up, dots, alphas) = refs
    else:
        (o_ref, q_ref, leg_high, leg_low, live, prior, old, direction, z_in, old_solution,
         residual, solution, spread_down, turned_down, tiles, alphas) = refs
    blocks = o_ref.shape[0]
    lanes = o_ref.shape[3]
    group = GROUP
    rows = residual.shape[1]

    @pl.when(s == 0)
    def _():
        for b in range(blocks):
            for h in range(2):
                spread_down[(2 * b + h) * half:(2 * b + h + 1) * half, :] = o_ref[b, h, 0:half]
        for k in range(tiles.shape[0]):
            tiles[k] = spread_down[k * lanes:(k + 1) * lanes, :].T
            for piece in range(group):
                turned_down[piece * rows // 2:(piece + 1) * rows // 2, k * lanes:(k + 1) * lanes] = tiles[
                    k, pl.ds(piece, rows // 2, stride=group), :
                ]
        if kind != "first":
            sums = sums_of(o_ref, half, group)
            scalars = q_ref[...]
            alpha = pick_row(scalars, 0) / (pick_row(sums, 0) + pick_row(scalars, 1))
            wanted = [alpha, pick_row(scalars, 2)] if kind == "last" else [alpha]
            for index, row in enumerate(wanted):
                tiles[0] = to_column(row)
                once = tiles[0, pl.ds(0, rows // 2, stride=group), :]
                alphas[index] = jnp.concatenate([once, once], axis=0)

    where = pl.ds(pl.multiple_of(s * rows, rows), rows)
    cycles = turned_down[where, :]
    image = product(cycles, leg_high[0], leg_low[0], NT)
    mask = live[0]
    if kind == "first":
        res = mask * image
    else:
        alpha = alphas[0, :, 0:1]
        d = direction[0]
        if kind == "last":
            d = z_in[0] + alphas[1, :, 0:1] * d
        image = mask * (image + prior[...] * d)
        res = old[0] - alpha * image
        if kind == "last":
            solution[0] = old_solution[0] + alpha * d
        else:
            solution[0] = alpha * d
    residual[0] = res
    if kind == "last":
        return
    z = mask * product(res, pre_high[0], pre_low[0], NN)
    z_out[0] = z
    pairs = [res * z, prior[...] * z * z]
    if kind == "middle":
        pairs.append(prior[...] * z * d)
    for index, pair in enumerate(pairs):
        dots[index, where, :] = jnp.broadcast_to(
            jnp.sum(pair, axis=1, keepdims=True), (rows, lanes)
        )
    up[where, :] = product(z, leg_high[0], leg_low[0], NN)

    @pl.when(s == pl.num_programs(0) - 1)
    def _():
        sums = []
        for index in range(len(pairs)):
            column = dots[index, 0:rows // 2]
            for piece in range(1, group):
                column = column + dots[index, piece * rows // 2:(piece + 1) * rows // 2]
            tiles[0] = jnp.zeros((lanes, lanes), jnp.float32)
            tiles[0, pl.ds(0, rows // 2, stride=group), :] = column
            sums.append(tiles[0].T[0:1])
        tile = tile_of(sums)
        for k in range(tiles.shape[0]):
            for piece in range(group):
                tiles[k, pl.ds(piece, rows // 2, stride=group), :] = up[
                    piece * rows // 2:(piece + 1) * rows // 2, k * lanes:(k + 1) * lanes
                ]
            spread_down[k * lanes:(k + 1) * lanes, :] = tiles[k].T
        for b in range(blocks):
            for h in range(2):
                at = (2 * b + h) * half
                p_ref[b, h, 0:half] = spread_down[at:at + half, :]
                p_ref[b, h, half:] = jnp.zeros((p_ref.shape[2] - half, lanes), jnp.float32)
            p_ref[b, 0, half:half + 8] = tile


def coeff_call(kind, cycle_count, lanes, *operands):
    legendre_at = 1 if kind == "first" else 2
    slots, degrees, cycles = operands[legendre_at].shape
    rows = lanes // slots
    blocks, _, padded, _ = operands[0].shape
    in_specs = []
    for place, operand in enumerate(operands):
        if place >= legendre_at and operand.ndim == 3:
            in_specs.append(pl.BlockSpec((1,) + operand.shape[1:], lambda s: (s, 0, 0)))
        else:
            in_specs.append(VMEM_WHOLE)
    vector = jax.ShapeDtypeStruct((slots, rows, degrees), jnp.float32)
    vector_spec = pl.BlockSpec((1, rows, degrees), lambda s: (s, 0, 0))
    partial = jax.ShapeDtypeStruct(operands[0].shape, jnp.float32)
    scratch = [
        pltpu.VMEM((cycles, lanes), jnp.float32),
        pltpu.VMEM((lanes, cycles), jnp.float32),
        pltpu.VMEM((cycles // lanes, lanes, lanes), jnp.float32),
    ]
    if kind == "last":
        out_shape, out_specs = [vector] * 2, [vector_spec] * 2
    else:
        vectors = 2 if kind == "first" else 3
        out_shape = [partial] + [vector] * vectors
        out_specs = [VMEM_WHOLE] + [vector_spec] * vectors
        scratch.append(pltpu.VMEM((lanes, cycles), jnp.float32))
        scratch.append(pltpu.VMEM((3, lanes, lanes), jnp.float32))
    if kind != "first":
        scratch.append(pltpu.VMEM((2, rows, lanes), jnp.float32))
    return pl.pallas_call(
        functools.partial(coeff_kernel, kind, cycle_count // 2),
        grid=(slots,),
        out_shape=out_shape,
        in_specs=in_specs,
        out_specs=out_specs,
        scratch_shapes=scratch,
        compiler_params=pltpu.CompilerParams(vmem_limit_bytes=60 << 20),
        name="coeff_" + kind,
    )(*operands)


def fast_body(anomalies, classes, legendre, precond, prior, assign):
    lon_count = lax.axis_size("lon")
    blocks = lax.axis_size("blk")
    blk_place = lax.axis_index("blk")
    lon_place = lax.axis_index("lon")
    slot_count, local_degrees, _ = legendre.shape
    rhs_count, cycle_count, longitudes = anomalies.shape
    window = assign.shape[0]
    block_width = precond.shape[2]
    lanes = slot_count * 2 * rhs_count
    stride_value = local_degrees * lon_count // window
    all_orders = assign * stride_value
    own_orders = lax.dynamic_slice_in_dim(all_orders, blk_place * slot_count, slot_count)
    live = build_mask(own_orders, lon_place * local_degrees, local_degrees)
    live = jnp.broadcast_to(live, (slot_count, 2, rhs_count, local_degrees)).reshape(
        slot_count, 2 * rhs_count, local_degrees
    )
    weights = huber_weights(classes)
    trig = trig_table(
        all_orders, lon_place * longitudes, longitudes, longitudes * lon_count
    ).reshape(2 * window, longitudes)
    trig_high, trig_rest = split_outside(trig)
    trig_up = jnp.concatenate([trig_high, trig_rest, trig_high], axis=0)
    trig_down = jnp.concatenate([trig_high, trig_rest], axis=0).T
    trig_low = jnp.concatenate([trig_high, jnp.zeros_like(trig_high)], axis=0).T
    leg = split_outside(legendre)
    per_slot = precond.shape[1]
    dense = precond[:, :, :, None, :] * jnp.eye(per_slot, dtype=jnp.float32)[None, :, None, :, None]
    pre = split_outside(dense.reshape(slot_count, local_degrees, local_degrees))
    prior_row = prior[None, :]
    on_grid = functools.partial(grid_call)

    sizes = (blocks, lanes, cycle_count, rhs_count)
    (partial,) = on_grid("data", *sizes, anomalies, weights, trig_down, trig_low)
    sums = exchange(partial)
    partial, residual, direction = coeff_call(
        "first", cycle_count, lanes, sums, *leg, *pre, live, prior_row
    )
    first_up = exchange(partial)
    partial, scalars = on_grid(
        "first", *sizes, first_up, weights, trig_up, trig_down, trig_low
    )
    sums = exchange(partial)
    partial, residual, search, solved = coeff_call(
        "middle", cycle_count, lanes, sums, scalars, *leg, *pre, live, prior_row,
        residual, direction,
    )
    second_up = exchange(partial)
    partial, scalars = on_grid(
        "next", *sizes, second_up, first_up, scalars, weights, trig_up, trig_down, trig_low
    )
    sums = exchange(partial)
    residual, solved = coeff_call(
        "last", cycle_count, lanes, sums, scalars, *leg, live, prior_row,
        residual, direction, search, solved,
    )
    shape = (slot_count, 2, rhs_count, local_degrees)
    return solved.reshape(shape), residual.reshape(shape)


def body(anomalies, classes, legendre, precond, prior, assign):
    fits = (
        lax.axis_size("lon") == 4
        and lax.axis_size("blk") % 2 == 0
        and anomalies.shape[1] % 16 == 0
        and legendre.shape[0] * 2 == GROUP
        and legendre.shape[2] % 128 == 0
        and legendre.shape[0] * 2 * anomalies.shape[0] == 128
    )
    chosen = fast_body if fits else plain_body
    return chosen(anomalies, classes, legendre, precond, prior, assign)


def solution(mesh):
    in_specs = (
        P(None, "blk", "lon"),
        P("blk", "lon"),
        P("blk", "lon", None),
        P("blk", "lon", None, None),
        P("lon"),
        P(),
    )
    out_specs = (P("blk", None, None, "lon"), P("blk", None, None, "lon"))
    return jax.shard_map(body, mesh=mesh, in_specs=in_specs, out_specs=out_specs, check_vma=False)
```

```python
import functools
import math

import jax
import jax.numpy as jnp
from jax import lax
from jax.experimental import pallas as pl
from jax.experimental.pallas import tpu as pltpu
from jax.sharding import PartitionSpec as P

ITERS = 2


HUBER_LEVELS = (1.0, 0.5, 0.25, 0.125)
HIGHEST = lax.Precision.HIGHEST
GROUP = 8
NEVER = 2**30
MESH = pl.DeviceIdType.MESH
VMEM_WHOLE = pl.BlockSpec(memory_space=pltpu.VMEM)


def build_mask(orders, first_degree, degrees):
    degree = first_degree + jnp.arange(degrees, dtype=jnp.int32)
    upper_part = (degree[None, :] >= orders[:, None]).astype(jnp.float32)
    sine_keep = upper_part * (orders[:, None] > 0).astype(jnp.float32)
    return jnp.stack([upper_part, sine_keep], axis=1)[:, :, None, :]


def trig_table(orders, first_col, columns, lon_total):
    column = first_col + jnp.arange(columns, dtype=jnp.int32)
    phases = orders[:, None] * column[None, :] % lon_total
    angles = phases.astype(jnp.float32) * (2.0 * math.pi / lon_total)
    return jnp.stack([jnp.cos(angles), jnp.sin(angles)], axis=1)


def huber_weights(classes):
    weighted = jnp.zeros(classes.shape, jnp.float32)
    for level_index in range(4):
        weighted = (
            weighted + (classes == level_index).astype(jnp.float32) * HUBER_LEVELS[level_index]
        )
    return weighted


def legendre_up(coeffs, basis_rows):
    return jnp.einsum("scnl,slr->scnr", coeffs, basis_rows, precision=HIGHEST)


def legendre_down(cycles_part, basis_rows):
    return jnp.einsum("scnr,slr->scnl", cycles_part, basis_rows, precision=HIGHEST)


def plain_body(anomalies, classes, legendre, precond, prior, assign):
    lon_count = lax.axis_size("lon")
    blk_count = lax.axis_size("blk")
    blk_place = lax.axis_index("blk")
    lon_place = lax.axis_index("lon")
    slot_count = legendre.shape[0]
    local_degrees = legendre.shape[1]
    rhs_count = anomalies.shape[0]
    cycle_count = anomalies.shape[1]
    longitudes = anomalies.shape[2]
    window = assign.shape[0]
    block_width = precond.shape[2]
    quarter = slot_count // lon_count
    grid_rows = rhs_count * cycle_count
    stride_value = local_degrees * lon_count // window
    all_orders = assign * stride_value
    own_orders = lax.dynamic_slice_in_dim(all_orders, blk_place * slot_count, slot_count)
    first_degree = lon_place * local_degrees
    first_column = lon_place * longitudes
    live_mask = build_mask(own_orders, first_degree, local_degrees)
    weights = huber_weights(classes)
    row_orders = (
        all_orders.reshape(blk_count, lon_count, quarter).transpose(1, 0, 2).reshape(window)
    )
    trig_rows = trig_table(row_orders, first_column, longitudes, longitudes * lon_count).reshape(
        2 * window, longitudes
    )

    def analyse(grid_field):
        flat_grid = grid_field.reshape(grid_rows, longitudes)
        product = lax.dot_general(trig_rows, flat_grid, (((1,), (1,)), ((), ())), precision=HIGHEST)
        shared = lax.psum_scatter(
            product.reshape(window // lon_count * lax.axis_size("lon"), 2, rhs_count, cycle_count),
            "lon",
            scatter_dimension=0,
            tiled=True,
        )
        returned = lax.all_to_all(shared, "blk", split_axis=0, concat_axis=3, tiled=True)
        return legendre_down(lax.all_gather(returned, "lon", axis=0, tiled=True), legendre)

    def precondition(coeffs):
        blocks = coeffs.reshape(slot_count, 2, rhs_count, local_degrees // block_width, block_width)
        applied = jnp.einsum("sbij,scnbj->scnbi", precond, blocks, precision=HIGHEST)
        return live_mask * applied.reshape(coeffs.shape)

    def column_dot(lhs_values, rhs_values):
        return jnp.sum(lhs_values * rhs_values, axis=(0, 1, 3))

    def spread(values):
        return values[None, None, :, None]

    def fit_sum(lhs_values, rhs_values):
        return lax.psum(column_dot(lhs_values, rhs_values), ("blk", "lon"))

    residual = live_mask * analyse(weights * anomalies)
    solution = jnp.zeros_like(residual)
    search = precondition(residual)
    fit_now = fit_sum(residual, search)
    direction = search
    for iteration in range(ITERS):
        synthesize_coeffs = direction
        synthesize_shared = lax.psum_scatter(
            legendre_up(synthesize_coeffs, legendre), "lon", scatter_dimension=0, tiled=True
        )
        moved = lax.all_to_all(synthesize_shared, "blk", split_axis=3, concat_axis=0, tiled=True)
        flat_orders = lax.all_gather(moved, "lon", axis=0, tiled=True).reshape(-1, grid_rows)
        grid_flat = lax.dot_general(
            flat_orders, trig_rows, (((0,), (0,)), ((), ())), precision=HIGHEST
        )
        image_vec = live_mask * (
            analyse(weights * grid_flat.reshape(rhs_count, cycle_count, longitudes))
            + prior * direction
        )
        curvature_sum = lax.psum(column_dot(direction, image_vec), ("blk", "lon"))
        alpha_step = fit_now / curvature_sum
        solution = solution + spread(alpha_step) * direction
        residual = residual - spread(alpha_step) * image_vec
        if iteration + 1 < ITERS:
            search = precondition(residual)
            fit_next = fit_sum(residual, search)
            direction = search + spread(fit_next / fit_now) * direction
            fit_now = fit_next
    return (solution, residual)


def split(values):
    high = values.astype(jnp.bfloat16)
    return high, (values - high.astype(jnp.float32)).astype(jnp.bfloat16)


def exchange_kernel(
    blocks, p_ref, o_ref, from_core, summed, from_x, ready, send_sem, recv_sem
):
    blk = lax.axis_index("blk")
    lon = lax.axis_index("lon")
    core, x = lon % 2, lon // 2
    core_mate = (blk, lon + 1 - 2 * core)
    x_mate = (blk, lon + 2 - 4 * x)
    part = from_x.shape[1]
    mine = pl.ds(pl.multiple_of(part * x, 8), part)
    theirs = pl.ds(pl.multiple_of(part * (1 - x), 8), part)
    barrier = pltpu.get_barrier_semaphore()
    peers = [core_mate, x_mate] + [((blk + j) % blocks, lon) for j in range(1, blocks)]
    for peer in peers:
        pl.semaphore_signal(barrier, inc=1, device_id=peer, device_id_type=MESH)
    pl.semaphore_wait(barrier, len(peers))

    def copy(stage, j, src, dst, peer):
        return pltpu.make_async_remote_copy(
            src_ref=src,
            dst_ref=dst,
            send_sem=send_sem.at[stage, j],
            recv_sem=recv_sem.at[stage, j],
            device_id=peer,
            device_id_type=MESH,
        )

    order = sorted(range(blocks), key=lambda j: (j == 0, abs(j - blocks // 2)))
    started = {}

    def launch(stage, j, src, dst, peer):
        started[stage, j] = copy(stage, j, src, dst, peer)
        started[stage, j].start()

    for j in order:
        to = (blk + j) % blocks
        launch(0, j, p_ref.at[to, 1 - core], from_core.at[to], core_mate)

    def over_x(j):
        to = (blk + j) % blocks
        started[0, j].wait_recv()
        summed[to] = p_ref[to, core] + from_core[to]
        launch(1, j, summed.at[to, theirs], from_x.at[to], x_mate)

    def over_blk(j):
        to = (blk + j) % blocks
        started[1, j].wait_recv()
        value = summed[to, mine] + from_x[to]
        if j == 0:
            o_ref[blk, core, mine] = value
        else:
            ready[to] = value
            launch(2, j, ready.at[to], o_ref.at[blk, core, mine], (to, lon))

    for j in order:
        over_x(j)
    for j in order:
        over_blk(j)
    arrivals = order[-1:] + order[:-1]
    for j in arrivals:
        source = (blk - j + blocks) % blocks
        if j:
            started[2, j].wait_recv()
        held = o_ref.at[source, core, mine]
        launch(3, j, held, held, x_mate)
        launch(4, j, held, held, core_mate)
    for j in arrivals:
        source = (blk - j + blocks) % blocks
        started[3, j].wait_recv()
        held = o_ref.at[source, core, theirs]
        launch(5, j, held, held, core_mate)
    for j in arrivals:
        started[4, j].wait_recv()
        started[5, j].wait_recv()
    for one in started.values():
        one.wait_send()


def exchange(partial):
    blocks, halves, padded, lanes = partial.shape
    return pl.pallas_call(
        functools.partial(exchange_kernel, blocks),
        out_shape=jax.ShapeDtypeStruct(partial.shape, jnp.float32),
        in_specs=[VMEM_WHOLE],
        out_specs=VMEM_WHOLE,
        scratch_shapes=[
            pltpu.VMEM((blocks, padded, lanes), jnp.float32),
            pltpu.VMEM((blocks, padded, lanes), jnp.float32),
            pltpu.VMEM((blocks, padded // 2, lanes), jnp.float32),
            pltpu.VMEM((blocks, padded // 2, lanes), jnp.float32),
            pltpu.SemaphoreType.DMA((6, blocks)),
            pltpu.SemaphoreType.DMA((6, blocks)),
        ],
        compiler_params=pltpu.CompilerParams(collective_id=0, has_side_effects=True),
        name="exchange",
    )(partial)


def group_sum(tile, group):
    lanes = tile.shape[1]
    at = lax.broadcasted_iota(jnp.int32, tile.shape, 1)
    shift = 1
    while shift < group:
        ahead = pltpu.roll(tile, lanes - shift, 1)
        behind = pltpu.roll(tile, shift, 1)
        tile = tile + jnp.where(at // shift % 2 == 0, ahead, behind)
        shift *= 2
    return tile


def sums_of(o_ref, half, group):
    tile = o_ref[0, 0, half:half + 8]
    for b in range(1, o_ref.shape[0]):
        tile = tile + o_ref[b, 0, half:half + 8]
    return group_sum(tile, group)


def pick_row(tile, row):
    return tile[row:row + 1]


def tile_of(rows):
    lanes = rows[0].shape[1]
    at = lax.broadcasted_iota(jnp.int32, (8, lanes), 0)
    tile = jnp.zeros((8, lanes), jnp.float32)
    for index, row in enumerate(rows):
        tile = jnp.where(at == index, jnp.broadcast_to(row, (8, lanes)), tile)
    return tile


def grid_kernel(kind, half, batch, *refs):
    steps = pl.num_programs(0)
    step = pl.program_id(0)
    if kind == "data":
        field, classes, trig, p_ref, weights, trig_up, trig_down, trig_low, down = refs
    elif kind == "first":
        o_ref, weights, trig_up, trig_down, trig_low, p_ref, q_ref, down, up, cycles = refs
    else:
        (o_ref, old_ref, old_q, weights, trig_up, trig_down, trig_low,
         p_ref, q_ref, down, up, cycles) = refs
    blocks, lanes = down.shape[0], down.shape[1]
    group = GROUP
    cycle_count = 2 * half
    if kind == "data":
        @pl.when(step == 0)
        def _():
            level = classes[...]
            weighted = jnp.zeros(level.shape, jnp.float32)
            for index, value in enumerate(HUBER_LEVELS):
                weighted = jnp.where(level == index, value, weighted)
            weights[...] = weighted
            table = trig[...]
            high = table.astype(jnp.bfloat16).astype(jnp.float32)
            rest = table - high
            trig_up[...] = jnp.concatenate([high, rest, high], axis=0).astype(jnp.bfloat16)
            trig_down[...] = jnp.concatenate([high, rest], axis=0).T.astype(jnp.bfloat16)
            trig_low[...] = (
                jnp.concatenate([high, jnp.zeros_like(high)], axis=0).T.astype(jnp.bfloat16)
            )
    else:
        @pl.when(step == 0)
        def _():
            sums = sums_of(o_ref, half, group)
            if kind == "first":
                q_ref[...] = sums
            else:
                before = old_q[...]
                beta = pick_row(sums, 0) / pick_row(before, 0)
                norm = (
                    pick_row(sums, 1)
                    + 2.0 * beta * pick_row(sums, 2)
                    + beta * beta * pick_row(before, 1)
                )
                q_ref[...] = tile_of([pick_row(sums, 0), norm, beta])
            for b in range(blocks):
                for h in range(2):
                    rows = o_ref[b, h, 0:half]
                    if kind != "first":
                        rows = rows + beta * old_ref[b, h, 0:half]
                    cycles[b, h * half:(h + 1) * half] = rows
                up[b] = cycles[b].T

    def place(inner):
        return pl.ds(pl.multiple_of((step * batch + inner) * group, 8), group)

    if kind == "data":
        grids = [field[inner] for inner in range(batch)]
    else:
        triples = []
        for inner in range(batch):
            stack = jnp.concatenate(
                [up[b, place(inner), :] for b in range(blocks)], axis=0
            )
            high = stack.astype(jnp.bfloat16).astype(jnp.float32)
            triple = jnp.concatenate([high, high, stack - high], axis=0)
            triples.append(triple.T.astype(jnp.bfloat16))
        fields = jnp.dot(
            jnp.concatenate(triples, axis=0), trig_up[...], preferred_element_type=jnp.float32
        )
        grids = [
            fields[inner * cycle_count:(inner + 1) * cycle_count] for inner in range(batch)
        ]
    scale = weights[...]
    parts = [split(one * scale) for one in grids]
    high = jnp.concatenate([part[0] for part in parts], axis=0)
    low = jnp.concatenate([part[1] for part in parts], axis=0)
    sums = jnp.dot(high, trig_down[...], preferred_element_type=jnp.float32)
    sums = sums + jnp.dot(low, trig_low[...], preferred_element_type=jnp.float32)
    for inner in range(batch):
        turned = sums[inner * cycle_count:(inner + 1) * cycle_count].T
        turned = turned[: group * blocks] + turned[group * blocks:]
        for b in range(blocks):
            down[b, place(inner), :] = turned[group * b:group * (b + 1)]

    @pl.when(step == steps - 1)
    def _():
        total = jnp.zeros((1, lanes), jnp.float32)
        for b in range(blocks):
            rows = down[b].T
            if kind != "data":
                total = total + jnp.sum(rows * cycles[b], axis=0, keepdims=True)
            for h in range(2):
                p_ref[b, h, 0:half] = rows[h * half:(h + 1) * half]
        for b in range(blocks):
            for h in range(2):
                p_ref[b, h, half:] = jnp.zeros((p_ref.shape[2] - half, lanes), jnp.float32)
            if kind != "data":
                p_ref[b, 0, half:half + 8] = tile_of([total])


def grid_call(kind, blocks, lanes, cycle_count, rhs_count, *operands):
    half = cycle_count // 2
    padded = -(-(half + 8) // 16) * 16
    batch = 4 if rhs_count % 4 == 0 else 1
    out_shape = [jax.ShapeDtypeStruct((blocks, 2, padded, lanes), jnp.float32)]
    scratch = [pltpu.VMEM((blocks, lanes, cycle_count), jnp.float32)]
    in_specs = [VMEM_WHOLE] * len(operands)
    if kind == "data":
        shape = operands[0].shape
        in_specs[0] = pl.BlockSpec((batch,) + shape[1:], lambda n: (n, 0, 0))
        rows = operands[2].shape[0]
        out_shape += [
            jax.ShapeDtypeStruct(shape[1:], jnp.float32),
            jax.ShapeDtypeStruct((3 * rows, shape[2]), jnp.bfloat16),
            jax.ShapeDtypeStruct((shape[2], 2 * rows), jnp.bfloat16),
            jax.ShapeDtypeStruct((shape[2], 2 * rows), jnp.bfloat16),
        ]
    else:
        out_shape.append(jax.ShapeDtypeStruct((8, lanes), jnp.float32))
        scratch.append(pltpu.VMEM((blocks, lanes, cycle_count), jnp.float32))
        scratch.append(pltpu.VMEM((blocks, cycle_count, lanes), jnp.float32))
    return pl.pallas_call(
        functools.partial(grid_kernel, kind, half, batch),
        grid=(rhs_count // batch,),
        out_shape=out_shape,
        in_specs=in_specs,
        out_specs=[VMEM_WHOLE] * len(out_shape),
        scratch_shapes=scratch,
        compiler_params=pltpu.CompilerParams(vmem_limit_bytes=60 << 20),
        name="grid_" + kind,
    )(*operands)


def to_column(row):
    return jnp.broadcast_to(row, (row.shape[1], row.shape[1])).T


def product(lhs, high, low, dims):
    lhs_high, lhs_low = split(lhs)
    rows = lhs.shape[0]
    both = jnp.concatenate([lhs_high, lhs_low], axis=0)
    first = lax.dot_general(both, high, dims, preferred_element_type=jnp.float32)
    second = lax.dot_general(lhs_high, low, dims, preferred_element_type=jnp.float32)
    return first[:rows] + first[rows:] + second


NN = (((1,), (0,)), ((), ()))
NT = (((1,), (1,)), ((), ()))


def block_diagonal(blocks_ref):
    _, count, width, _ = blocks_ref.shape
    rows = []
    for index in range(count):
        parts = []
        if index:
            parts.append(jnp.zeros((width, width * index), jnp.float32))
        parts.append(blocks_ref[0, index])
        if index + 1 < count:
            parts.append(jnp.zeros((width, width * (count - 1 - index)), jnp.float32))
        rows.append(jnp.concatenate(parts, axis=1))
    return jnp.concatenate(rows, axis=0)


def coeff_kernel(kind, half, *refs):
    s = pl.program_id(0)
    if kind == "first":
        (o_ref, places, legendre, precond, prior,
         p_ref, residual, z_out, leg_high, leg_low, pre_high, pre_low,
         spread_down, turned_down, tiles, up, dots) = refs
    elif kind == "middle":
        (o_ref, q_ref, leg_high, leg_low, pre_high, pre_low, places, prior, old, direction,
         p_ref, residual, z_out, solution, spread_down, turned_down, tiles, up, dots, alphas) = refs
    else:
        (o_ref, q_ref, leg_high, leg_low, places, prior, old, direction, z_in, old_solution,
         residual, solution, spread_down, turned_down, tiles, alphas) = refs
    blocks = o_ref.shape[0]
    lanes = o_ref.shape[3]
    group = GROUP
    rows = residual.shape[1]

    @pl.when(s == 0)
    def _():
        for b in range(blocks):
            for h in range(2):
                spread_down[(2 * b + h) * half:(2 * b + h + 1) * half, :] = o_ref[b, h, 0:half]
        for k in range(tiles.shape[0]):
            tiles[k] = spread_down[k * lanes:(k + 1) * lanes, :].T
            for piece in range(group):
                turned_down[piece * rows // 2:(piece + 1) * rows // 2, k * lanes:(k + 1) * lanes] = tiles[
                    k, pl.ds(piece, rows // 2, stride=group), :
                ]
        if kind != "first":
            sums = sums_of(o_ref, half, group)
            scalars = q_ref[...]
            alpha = pick_row(scalars, 0) / (pick_row(sums, 0) + pick_row(scalars, 1))
            wanted = [alpha, pick_row(scalars, 2)] if kind == "last" else [alpha]
            for index, row in enumerate(wanted):
                tiles[0] = to_column(row)
                once = tiles[0, pl.ds(0, rows // 2, stride=group), :]
                alphas[index] = jnp.concatenate([once, once], axis=0)

    where = pl.ds(pl.multiple_of(s * rows, rows), rows)
    if kind == "first":
        leg_high[0], leg_low[0] = split(legendre[0])
        pre_high[0], pre_low[0] = split(block_diagonal(precond))
    cycles = turned_down[where, :]
    image = product(cycles, leg_high[0], leg_low[0], NT)
    order = places[s]
    degree = places[pl.num_programs(0)] + lax.broadcasted_iota(jnp.int32, residual.shape[1:], 1)
    sine = lax.broadcasted_iota(jnp.int32, residual.shape[1:], 0) >= rows // 2
    least = jnp.where(sine, jnp.maximum(order, jnp.where(order == 0, NEVER, 0)), order)
    mask = (degree >= least).astype(jnp.float32)
    if kind == "first":
        res = mask * image
    else:
        alpha = alphas[0, :, 0:1]
        d = direction[0]
        if kind == "last":
            d = z_in[0] + alphas[1, :, 0:1] * d
        image = mask * (image + prior[...] * d)
        res = old[0] - alpha * image
        if kind == "last":
            solution[0] = old_solution[0] + alpha * d
        else:
            solution[0] = alpha * d
    residual[0] = res
    if kind == "last":
        return
    z = mask * product(res, pre_high[0], pre_low[0], NN)
    z_out[0] = z
    pairs = [res * z, prior[...] * z * z]
    if kind == "middle":
        pairs.append(prior[...] * z * d)
    for index, pair in enumerate(pairs):
        dots[index, where, :] = jnp.broadcast_to(
            jnp.sum(pair, axis=1, keepdims=True), (rows, lanes)
        )
    up[where, :] = product(z, leg_high[0], leg_low[0], NN)

    @pl.when(s == pl.num_programs(0) - 1)
    def _():
        sums = []
        for index in range(len(pairs)):
            column = dots[index, 0:rows // 2]
            for piece in range(1, group):
                column = column + dots[index, piece * rows // 2:(piece + 1) * rows // 2]
            tiles[0] = jnp.zeros((lanes, lanes), jnp.float32)
            tiles[0, pl.ds(0, rows // 2, stride=group), :] = column
            sums.append(tiles[0].T[0:1])
        tile = tile_of(sums)
        for k in range(tiles.shape[0]):
            for piece in range(group):
                tiles[k, pl.ds(piece, rows // 2, stride=group), :] = up[
                    piece * rows // 2:(piece + 1) * rows // 2, k * lanes:(k + 1) * lanes
                ]
            spread_down[k * lanes:(k + 1) * lanes, :] = tiles[k].T
        for b in range(blocks):
            for h in range(2):
                at = (2 * b + h) * half
                p_ref[b, h, 0:half] = spread_down[at:at + half, :]
                p_ref[b, h, half:] = jnp.zeros((p_ref.shape[2] - half, lanes), jnp.float32)
            p_ref[b, 0, half:half + 8] = tile


def coeff_call(kind, cycle_count, lanes, *operands):
    legendre_at = 2
    slots, degrees, cycles = operands[legendre_at].shape
    rows = lanes // slots
    blocks, _, padded, _ = operands[0].shape
    in_specs = []
    for place, operand in enumerate(operands):
        if place >= legendre_at and operand.ndim == 3:
            in_specs.append(pl.BlockSpec((1,) + operand.shape[1:], lambda s: (s, 0, 0)))
        elif place >= legendre_at and operand.ndim == 4:
            in_specs.append(pl.BlockSpec((1,) + operand.shape[1:], lambda s: (s, 0, 0, 0)))
        elif operand.ndim == 1:
            in_specs.append(pl.BlockSpec(memory_space=pltpu.SMEM))
        else:
            in_specs.append(VMEM_WHOLE)
    vector = jax.ShapeDtypeStruct((slots, rows, degrees), jnp.float32)
    vector_spec = pl.BlockSpec((1, rows, degrees), lambda s: (s, 0, 0))
    partial = jax.ShapeDtypeStruct(operands[0].shape, jnp.float32)
    scratch = [
        pltpu.VMEM((cycles, lanes), jnp.float32),
        pltpu.VMEM((lanes, cycles), jnp.float32),
        pltpu.VMEM((cycles // lanes, lanes, lanes), jnp.float32),
    ]
    if kind == "last":
        out_shape, out_specs = [vector] * 2, [vector_spec] * 2
    else:
        vectors = 2 if kind == "first" else 3
        out_shape = [partial] + [vector] * vectors
        out_specs = [VMEM_WHOLE] + [vector_spec] * vectors
        if kind == "first":
            for shape in ((degrees, cycles), (degrees, degrees)):
                out_shape += [jax.ShapeDtypeStruct((slots,) + shape, jnp.bfloat16)] * 2
                out_specs += [pl.BlockSpec((1,) + shape, lambda s: (s, 0, 0))] * 2
        scratch.append(pltpu.VMEM((lanes, cycles), jnp.float32))
        scratch.append(pltpu.VMEM((3, lanes, lanes), jnp.float32))
    if kind != "first":
        scratch.append(pltpu.VMEM((2, rows, lanes), jnp.float32))
    return pl.pallas_call(
        functools.partial(coeff_kernel, kind, cycle_count // 2),
        grid=(slots,),
        out_shape=out_shape,
        in_specs=in_specs,
        out_specs=out_specs,
        scratch_shapes=scratch,
        compiler_params=pltpu.CompilerParams(vmem_limit_bytes=60 << 20),
        name="coeff_" + kind,
    )(*operands)


def fast_body(anomalies, classes, legendre, precond, prior, assign):
    lon_count = lax.axis_size("lon")
    blocks = lax.axis_size("blk")
    blk_place = lax.axis_index("blk")
    lon_place = lax.axis_index("lon")
    slot_count, local_degrees, _ = legendre.shape
    rhs_count, cycle_count, longitudes = anomalies.shape
    window = assign.shape[0]
    block_width = precond.shape[2]
    lanes = slot_count * 2 * rhs_count
    stride_value = local_degrees * lon_count // window
    all_orders = assign * stride_value
    own_orders = lax.dynamic_slice_in_dim(all_orders, blk_place * slot_count, slot_count)
    places = jnp.concatenate([own_orders, (lon_place * local_degrees)[None]])
    pair_orders = jnp.repeat(all_orders, 2)[:, None]
    column = lon_place * longitudes + jnp.arange(longitudes, dtype=jnp.int32)
    phases = pair_orders * column[None, :] % (longitudes * lon_count)
    angles = phases.astype(jnp.float32) * (2.0 * math.pi / (longitudes * lon_count))
    sine = (jnp.arange(2 * window) % 2 == 1)[:, None]
    trig = jnp.where(sine, jnp.sin(angles), jnp.cos(angles))
    prior_row = prior[None, :]

    sizes = (blocks, lanes, cycle_count, rhs_count)
    partial, *tables = grid_call("data", *sizes, anomalies, classes, trig)
    sums = exchange(partial)
    partial, residual, direction, *factors = coeff_call(
        "first", cycle_count, lanes, sums, places, legendre, precond, prior_row
    )
    first_up = exchange(partial)
    partial, scalars = grid_call(
        "first", *sizes, first_up, *tables
    )
    sums = exchange(partial)
    partial, residual, search, solved = coeff_call(
        "middle", cycle_count, lanes, sums, scalars, *factors, places, prior_row,
        residual, direction,
    )
    second_up = exchange(partial)
    partial, scalars = grid_call(
        "next", *sizes, second_up, first_up, scalars, *tables
    )
    sums = exchange(partial)
    residual, solved = coeff_call(
        "last", cycle_count, lanes, sums, scalars, *factors[:2], places, prior_row,
        residual, direction, search, solved,
    )
    shape = (slot_count, 2, rhs_count, local_degrees)
    return solved.reshape(shape), residual.reshape(shape)


def body(anomalies, classes, legendre, precond, prior, assign):
    fits = (
        lax.axis_size("lon") == 4
        and lax.axis_size("blk") % 2 == 0
        and anomalies.shape[1] % 16 == 0
        and legendre.shape[0] * 2 == GROUP
        and legendre.shape[2] % 128 == 0
        and legendre.shape[0] * 2 * anomalies.shape[0] == 128
    )
    chosen = fast_body if fits else plain_body
    return chosen(anomalies, classes, legendre, precond, prior, assign)


def solution(mesh):
    in_specs = (
        P(None, "blk", "lon"),
        P("blk", "lon"),
        P("blk", "lon", None),
        P("blk", "lon", None, None),
        P("lon"),
        P(),
    )
    out_specs = (P("blk", None, None, "lon"), P("blk", None, None, "lon"))
    return jax.shard_map(body, mesh=mesh, in_specs=in_specs, out_specs=out_specs, check_vma=False)
```

```python
import functools
import math

import jax
import jax.numpy as jnp
from jax import lax
from jax.experimental import pallas as pl
from jax.experimental.pallas import tpu as pltpu
from jax.sharding import PartitionSpec as P

ITERS = 2


HUBER_LEVELS = (1.0, 0.5, 0.25, 0.125)
HIGHEST = lax.Precision.HIGHEST
GROUP = 8
NEVER = 2**30
MESH = pl.DeviceIdType.MESH
VMEM_WHOLE = pl.BlockSpec(memory_space=pltpu.VMEM)


def build_mask(orders, first_degree, degrees):
    degree = first_degree + jnp.arange(degrees, dtype=jnp.int32)
    upper_part = (degree[None, :] >= orders[:, None]).astype(jnp.float32)
    sine_keep = upper_part * (orders[:, None] > 0).astype(jnp.float32)
    return jnp.stack([upper_part, sine_keep], axis=1)[:, :, None, :]


def trig_table(orders, first_col, columns, lon_total):
    column = first_col + jnp.arange(columns, dtype=jnp.int32)
    phases = orders[:, None] * column[None, :] % lon_total
    angles = phases.astype(jnp.float32) * (2.0 * math.pi / lon_total)
    return jnp.stack([jnp.cos(angles), jnp.sin(angles)], axis=1)


def huber_weights(classes):
    weighted = jnp.zeros(classes.shape, jnp.float32)
    for level_index in range(4):
        weighted = (
            weighted + (classes == level_index).astype(jnp.float32) * HUBER_LEVELS[level_index]
        )
    return weighted


def legendre_up(coeffs, basis_rows):
    return jnp.einsum("scnl,slr->scnr", coeffs, basis_rows, precision=HIGHEST)


def legendre_down(cycles_part, basis_rows):
    return jnp.einsum("scnr,slr->scnl", cycles_part, basis_rows, precision=HIGHEST)


def plain_body(anomalies, classes, legendre, precond, prior, assign):
    lon_count = lax.axis_size("lon")
    blk_count = lax.axis_size("blk")
    blk_place = lax.axis_index("blk")
    lon_place = lax.axis_index("lon")
    slot_count = legendre.shape[0]
    local_degrees = legendre.shape[1]
    rhs_count = anomalies.shape[0]
    cycle_count = anomalies.shape[1]
    longitudes = anomalies.shape[2]
    window = assign.shape[0]
    block_width = precond.shape[2]
    quarter = slot_count // lon_count
    grid_rows = rhs_count * cycle_count
    stride_value = local_degrees * lon_count // window
    all_orders = assign * stride_value
    own_orders = lax.dynamic_slice_in_dim(all_orders, blk_place * slot_count, slot_count)
    first_degree = lon_place * local_degrees
    first_column = lon_place * longitudes
    live_mask = build_mask(own_orders, first_degree, local_degrees)
    weights = huber_weights(classes)
    row_orders = (
        all_orders.reshape(blk_count, lon_count, quarter).transpose(1, 0, 2).reshape(window)
    )
    trig_rows = trig_table(row_orders, first_column, longitudes, longitudes * lon_count).reshape(
        2 * window, longitudes
    )

    def analyse(grid_field):
        flat_grid = grid_field.reshape(grid_rows, longitudes)
        product = lax.dot_general(trig_rows, flat_grid, (((1,), (1,)), ((), ())), precision=HIGHEST)
        shared = lax.psum_scatter(
            product.reshape(window // lon_count * lax.axis_size("lon"), 2, rhs_count, cycle_count),
            "lon",
            scatter_dimension=0,
            tiled=True,
        )
        returned = lax.all_to_all(shared, "blk", split_axis=0, concat_axis=3, tiled=True)
        return legendre_down(lax.all_gather(returned, "lon", axis=0, tiled=True), legendre)

    def precondition(coeffs):
        blocks = coeffs.reshape(slot_count, 2, rhs_count, local_degrees // block_width, block_width)
        applied = jnp.einsum("sbij,scnbj->scnbi", precond, blocks, precision=HIGHEST)
        return live_mask * applied.reshape(coeffs.shape)

    def column_dot(lhs_values, rhs_values):
        return jnp.sum(lhs_values * rhs_values, axis=(0, 1, 3))

    def spread(values):
        return values[None, None, :, None]

    def fit_sum(lhs_values, rhs_values):
        return lax.psum(column_dot(lhs_values, rhs_values), ("blk", "lon"))

    residual = live_mask * analyse(weights * anomalies)
    solution = jnp.zeros_like(residual)
    search = precondition(residual)
    fit_now = fit_sum(residual, search)
    direction = search
    for iteration in range(ITERS):
        synthesize_coeffs = direction
        synthesize_shared = lax.psum_scatter(
            legendre_up(synthesize_coeffs, legendre), "lon", scatter_dimension=0, tiled=True
        )
        moved = lax.all_to_all(synthesize_shared, "blk", split_axis=3, concat_axis=0, tiled=True)
        flat_orders = lax.all_gather(moved, "lon", axis=0, tiled=True).reshape(-1, grid_rows)
        grid_flat = lax.dot_general(
            flat_orders, trig_rows, (((0,), (0,)), ((), ())), precision=HIGHEST
        )
        image_vec = live_mask * (
            analyse(weights * grid_flat.reshape(rhs_count, cycle_count, longitudes))
            + prior * direction
        )
        curvature_sum = lax.psum(column_dot(direction, image_vec), ("blk", "lon"))
        alpha_step = fit_now / curvature_sum
        solution = solution + spread(alpha_step) * direction
        residual = residual - spread(alpha_step) * image_vec
        if iteration + 1 < ITERS:
            search = precondition(residual)
            fit_next = fit_sum(residual, search)
            direction = search + spread(fit_next / fit_now) * direction
            fit_now = fit_next
    return (solution, residual)


def split(values):
    high = values.astype(jnp.bfloat16)
    return high, (values - high.astype(jnp.float32)).astype(jnp.bfloat16)


def mates():
    blk = lax.axis_index("blk")
    lon = lax.axis_index("lon")
    core, x = lon % 2, lon // 2
    return blk, lon, core, x, (blk, lon + 1 - 2 * core), (blk, lon + 2 - 4 * x)


def greet(blocks):
    blk, lon, _, _, core_mate, x_mate = mates()
    barrier = pltpu.get_barrier_semaphore()
    peers = [core_mate, x_mate] + [((blk + j) % blocks, lon) for j in range(1, blocks)]
    for peer in peers:
        pl.semaphore_signal(barrier, inc=1, device_id=peer, device_id_type=MESH)


def exchange(blocks, p_ref, landed, from_core, summed, from_x, ready, send_sem, recv_sem):
    blk, lon, core, x, core_mate, x_mate = mates()
    o_ref = landed
    pl.semaphore_wait(pltpu.get_barrier_semaphore(), blocks + 1)
    part = from_x.shape[1]
    mine = pl.ds(pl.multiple_of(part * x, 8), part)
    theirs = pl.ds(pl.multiple_of(part * (1 - x), 8), part)

    def copy(stage, j, src, dst, peer):
        return pltpu.make_async_remote_copy(
            src_ref=src,
            dst_ref=dst,
            send_sem=send_sem.at[stage, j],
            recv_sem=recv_sem.at[stage, j],
            device_id=peer,
            device_id_type=MESH,
        )

    order = sorted(range(blocks), key=lambda j: (j == 0, abs(j - blocks // 2)))
    started = {}

    def launch(stage, j, src, dst, peer):
        started[stage, j] = copy(stage, j, src, dst, peer)
        started[stage, j].start()

    for j in order:
        to = (blk + j) % blocks
        launch(0, j, p_ref.at[to, 1 - core], from_core.at[to], core_mate)

    def over_x(j):
        to = (blk + j) % blocks
        started[0, j].wait_recv()
        summed[to] = p_ref[to, core] + from_core[to]
        launch(1, j, summed.at[to, theirs], from_x.at[to], x_mate)

    def over_blk(j):
        to = (blk + j) % blocks
        started[1, j].wait_recv()
        value = summed[to, mine] + from_x[to]
        if j == 0:
            o_ref[blk, core, mine] = value
        else:
            ready[to] = value
            launch(2, j, ready.at[to], o_ref.at[blk, core, mine], (to, lon))

    for j in order:
        over_x(j)
    for j in order:
        over_blk(j)
    arrivals = order[-1:] + order[:-1]
    for j in arrivals:
        source = (blk - j + blocks) % blocks
        if j:
            started[2, j].wait_recv()
        held = o_ref.at[source, core, mine]
        launch(3, j, held, held, x_mate)
        launch(4, j, held, held, core_mate)
    for j in arrivals:
        source = (blk - j + blocks) % blocks
        started[3, j].wait_recv()
        held = o_ref.at[source, core, theirs]
        launch(5, j, held, held, core_mate)
    for j in arrivals:
        started[4, j].wait_recv()
        started[5, j].wait_recv()
    for one in started.values():
        one.wait_send()


def exchange_scratch(blocks, padded, lanes):
    return [
        pltpu.VMEM((blocks, 2, padded, lanes), jnp.float32),
        pltpu.VMEM((blocks, 2, padded, lanes), jnp.float32),
        pltpu.VMEM((blocks, padded, lanes), jnp.float32),
        pltpu.VMEM((blocks, padded, lanes), jnp.float32),
        pltpu.VMEM((blocks, padded // 2, lanes), jnp.float32),
        pltpu.VMEM((blocks, padded // 2, lanes), jnp.float32),
        pltpu.SemaphoreType.DMA((6, blocks)),
        pltpu.SemaphoreType.DMA((6, blocks)),
    ]


def group_sum(tile, group):
    lanes = tile.shape[1]
    at = lax.broadcasted_iota(jnp.int32, tile.shape, 1)
    shift = 1
    while shift < group:
        ahead = pltpu.roll(tile, lanes - shift, 1)
        behind = pltpu.roll(tile, shift, 1)
        tile = tile + jnp.where(at // shift % 2 == 0, ahead, behind)
        shift *= 2
    return tile


def sums_of(o_ref, half, group):
    tile = o_ref[0, 0, half:half + 8]
    for b in range(1, o_ref.shape[0]):
        tile = tile + o_ref[b, 0, half:half + 8]
    return group_sum(tile, group)


def pick_row(tile, row):
    return tile[row:row + 1]


def tile_of(rows):
    lanes = rows[0].shape[1]
    at = lax.broadcasted_iota(jnp.int32, (8, lanes), 0)
    tile = jnp.zeros((8, lanes), jnp.float32)
    for index, row in enumerate(rows):
        tile = jnp.where(at == index, jnp.broadcast_to(row, (8, lanes)), tile)
    return tile


def grid_kernel(kind, half, batch, *refs):
    steps = pl.num_programs(0)
    step = pl.program_id(0)
    refs, p_ref, links = refs[:-8], refs[-8], refs[-7:]
    if kind == "data":
        field, classes, trig, out_ref, weights, trig_up, trig_down, trig_low, down = refs
    elif kind == "first":
        o_ref, weights, trig_up, trig_down, trig_low, out_ref, q_ref, down, up, cycles = refs
    else:
        (o_ref, old_ref, old_q, weights, trig_up, trig_down, trig_low,
         out_ref, q_ref, down, up, cycles) = refs
    blocks, lanes = down.shape[0], down.shape[1]
    group = GROUP
    cycle_count = 2 * half

    @pl.when(step == 0)
    def _():
        greet(blocks)

    if kind == "data":
        @pl.when(step == 0)
        def _():
            level = classes[...]
            weighted = jnp.zeros(level.shape, jnp.float32)
            for index, value in enumerate(HUBER_LEVELS):
                weighted = jnp.where(level == index, value, weighted)
            weights[...] = weighted
            table = trig[...]
            high = table.astype(jnp.bfloat16).astype(jnp.float32)
            rest = table - high
            trig_up[...] = jnp.concatenate([high, rest, high], axis=0).astype(jnp.bfloat16)
            trig_down[...] = jnp.concatenate([high, rest], axis=0).T.astype(jnp.bfloat16)
            trig_low[...] = (
                jnp.concatenate([high, jnp.zeros_like(high)], axis=0).T.astype(jnp.bfloat16)
            )
    else:
        @pl.when(step == 0)
        def _():
            sums = sums_of(o_ref, half, group)
            if kind == "first":
                q_ref[...] = sums
            else:
                before = old_q[...]
                beta = pick_row(sums, 0) / pick_row(before, 0)
                norm = (
                    pick_row(sums, 1)
                    + 2.0 * beta * pick_row(sums, 2)
                    + beta * beta * pick_row(before, 1)
                )
                q_ref[...] = tile_of([pick_row(sums, 0), norm, beta])
            for b in range(blocks):
                for h in range(2):
                    rows = o_ref[b, h, 0:half]
                    if kind != "first":
                        rows = rows + beta * old_ref[b, h, 0:half]
                    cycles[b, h * half:(h + 1) * half] = rows
                up[b] = cycles[b].T

    def place(inner):
        return pl.ds(pl.multiple_of((step * batch + inner) * group, 8), group)

    if kind == "data":
        grids = [field[inner] for inner in range(batch)]
    else:
        triples = []
        for inner in range(batch):
            stack = jnp.concatenate(
                [up[b, place(inner), :] for b in range(blocks)], axis=0
            )
            high = stack.astype(jnp.bfloat16).astype(jnp.float32)
            triple = jnp.concatenate([high, high, stack - high], axis=0)
            triples.append(triple.T.astype(jnp.bfloat16))
        fields = jnp.dot(
            jnp.concatenate(triples, axis=0), trig_up[...], preferred_element_type=jnp.float32
        )
        grids = [
            fields[inner * cycle_count:(inner + 1) * cycle_count] for inner in range(batch)
        ]
    scale = weights[...]
    parts = [split(one * scale) for one in grids]
    high = jnp.concatenate([part[0] for part in parts], axis=0)
    low = jnp.concatenate([part[1] for part in parts], axis=0)
    sums = jnp.dot(high, trig_down[...], preferred_element_type=jnp.float32)
    sums = sums + jnp.dot(low, trig_low[...], preferred_element_type=jnp.float32)
    for inner in range(batch):
        turned = sums[inner * cycle_count:(inner + 1) * cycle_count].T
        turned = turned[: group * blocks] + turned[group * blocks:]
        for b in range(blocks):
            down[b, place(inner), :] = turned[group * b:group * (b + 1)]

    @pl.when(step == steps - 1)
    def _():
        total = jnp.zeros((1, lanes), jnp.float32)
        for b in range(blocks):
            rows = down[b].T
            if kind != "data":
                total = total + jnp.sum(rows * cycles[b], axis=0, keepdims=True)
            for h in range(2):
                p_ref[b, h, 0:half] = rows[h * half:(h + 1) * half]
        for b in range(blocks):
            for h in range(2):
                p_ref[b, h, half:] = jnp.zeros((p_ref.shape[2] - half, lanes), jnp.float32)
            if kind != "data":
                p_ref[b, 0, half:half + 8] = tile_of([total])
        exchange(blocks, p_ref, *links)
        for b in range(blocks):
            out_ref[b] = links[0][b]


def grid_call(kind, blocks, lanes, cycle_count, rhs_count, *operands):
    half = cycle_count // 2
    padded = -(-(half + 8) // 16) * 16
    batch = 4 if rhs_count % 4 == 0 else 1
    out_shape = [jax.ShapeDtypeStruct((blocks, 2, padded, lanes), jnp.float32)]
    scratch = [pltpu.VMEM((blocks, lanes, cycle_count), jnp.float32)]
    in_specs = [VMEM_WHOLE] * len(operands)
    if kind == "data":
        shape = operands[0].shape
        in_specs[0] = pl.BlockSpec((batch,) + shape[1:], lambda n: (n, 0, 0))
        rows = operands[2].shape[0]
        out_shape += [
            jax.ShapeDtypeStruct(shape[1:], jnp.float32),
            jax.ShapeDtypeStruct((3 * rows, shape[2]), jnp.bfloat16),
            jax.ShapeDtypeStruct((shape[2], 2 * rows), jnp.bfloat16),
            jax.ShapeDtypeStruct((shape[2], 2 * rows), jnp.bfloat16),
        ]
    else:
        out_shape.append(jax.ShapeDtypeStruct((8, lanes), jnp.float32))
        scratch.append(pltpu.VMEM((blocks, lanes, cycle_count), jnp.float32))
        scratch.append(pltpu.VMEM((blocks, cycle_count, lanes), jnp.float32))
    scratch += exchange_scratch(blocks, padded, lanes)
    return pl.pallas_call(
        functools.partial(grid_kernel, kind, half, batch),
        grid=(rhs_count // batch,),
        out_shape=out_shape,
        in_specs=in_specs,
        out_specs=[VMEM_WHOLE] * len(out_shape),
        scratch_shapes=scratch,
        compiler_params=pltpu.CompilerParams(
            vmem_limit_bytes=60 << 20,
            collective_id=("data", "first", "next").index(kind),
            has_side_effects=True,
        ),
        name="grid_" + kind,
    )(*operands)


def to_column(row):
    return jnp.broadcast_to(row, (row.shape[1], row.shape[1])).T


def product(lhs, high, low, dims):
    lhs_high, lhs_low = split(lhs)
    rows = lhs.shape[0]
    both = jnp.concatenate([lhs_high, lhs_low], axis=0)
    first = lax.dot_general(both, high, dims, preferred_element_type=jnp.float32)
    second = lax.dot_general(lhs_high, low, dims, preferred_element_type=jnp.float32)
    return first[:rows] + first[rows:] + second


NN = (((1,), (0,)), ((), ()))
NT = (((1,), (1,)), ((), ()))


def block_diagonal(blocks_ref):
    _, count, width, _ = blocks_ref.shape
    rows = []
    for index in range(count):
        parts = []
        if index:
            parts.append(jnp.zeros((width, width * index), jnp.float32))
        parts.append(blocks_ref[0, index])
        if index + 1 < count:
            parts.append(jnp.zeros((width, width * (count - 1 - index)), jnp.float32))
        rows.append(jnp.concatenate(parts, axis=1))
    return jnp.concatenate(rows, axis=0)


def coeff_kernel(kind, half, *refs):
    s = pl.program_id(0)
    if kind != "last":
        refs, p_ref, links = refs[:-8], refs[-8], refs[-7:]
    if kind == "first":
        (o_ref, places, legendre, precond, prior,
         out_ref, residual, z_out, leg_high, leg_low, pre_high, pre_low,
         spread_down, turned_down, tiles, up, dots) = refs
    elif kind == "middle":
        (o_ref, q_ref, leg_high, leg_low, pre_high, pre_low, places, prior, old, direction,
         out_ref, residual, z_out, solution, spread_down, turned_down, tiles, up, dots, alphas) = refs
    else:
        (o_ref, q_ref, leg_high, leg_low, places, prior, old, direction, z_in, old_solution,
         residual, solution, spread_down, turned_down, tiles, alphas) = refs
    blocks = o_ref.shape[0]
    lanes = o_ref.shape[3]
    group = GROUP
    rows = residual.shape[1]

    @pl.when(s == 0)
    def _():
        if kind != "last":
            greet(blocks)
        for b in range(blocks):
            for h in range(2):
                spread_down[(2 * b + h) * half:(2 * b + h + 1) * half, :] = o_ref[b, h, 0:half]
        for k in range(tiles.shape[0]):
            tiles[k] = spread_down[k * lanes:(k + 1) * lanes, :].T
            for piece in range(group):
                turned_down[piece * rows // 2:(piece + 1) * rows // 2, k * lanes:(k + 1) * lanes] = tiles[
                    k, pl.ds(piece, rows // 2, stride=group), :
                ]
        if kind != "first":
            sums = sums_of(o_ref, half, group)
            scalars = q_ref[...]
            alpha = pick_row(scalars, 0) / (pick_row(sums, 0) + pick_row(scalars, 1))
            wanted = [alpha, pick_row(scalars, 2)] if kind == "last" else [alpha]
            for index, row in enumerate(wanted):
                tiles[0] = to_column(row)
                once = tiles[0, pl.ds(0, rows // 2, stride=group), :]
                alphas[index] = jnp.concatenate([once, once], axis=0)

    where = pl.ds(pl.multiple_of(s * rows, rows), rows)
    if kind == "first":
        leg_high[0], leg_low[0] = split(legendre[0])
        pre_high[0], pre_low[0] = split(block_diagonal(precond))
    cycles = turned_down[where, :]
    image = product(cycles, leg_high[0], leg_low[0], NT)
    order = places[s]
    degree = places[pl.num_programs(0)] + lax.broadcasted_iota(jnp.int32, residual.shape[1:], 1)
    sine = lax.broadcasted_iota(jnp.int32, residual.shape[1:], 0) >= rows // 2
    least = jnp.where(sine, jnp.maximum(order, jnp.where(order == 0, NEVER, 0)), order)
    mask = (degree >= least).astype(jnp.float32)
    if kind == "first":
        res = mask * image
    else:
        alpha = alphas[0, :, 0:1]
        d = direction[0]
        if kind == "last":
            d = z_in[0] + alphas[1, :, 0:1] * d
        image = mask * (image + prior[...] * d)
        res = old[0] - alpha * image
        if kind == "last":
            solution[0] = old_solution[0] + alpha * d
        else:
            solution[0] = alpha * d
    residual[0] = res
    if kind == "last":
        return
    z = mask * product(res, pre_high[0], pre_low[0], NN)
    z_out[0] = z
    pairs = [res * z, prior[...] * z * z]
    if kind == "middle":
        pairs.append(prior[...] * z * d)
    for index, pair in enumerate(pairs):
        dots[index, where, :] = jnp.broadcast_to(
            jnp.sum(pair, axis=1, keepdims=True), (rows, lanes)
        )
    up[where, :] = product(z, leg_high[0], leg_low[0], NN)

    @pl.when(s == pl.num_programs(0) - 1)
    def _():
        sums = []
        for index in range(len(pairs)):
            column = dots[index, 0:rows // 2]
            for piece in range(1, group):
                column = column + dots[index, piece * rows // 2:(piece + 1) * rows // 2]
            tiles[0] = jnp.zeros((lanes, lanes), jnp.float32)
            tiles[0, pl.ds(0, rows // 2, stride=group), :] = column
            sums.append(tiles[0].T[0:1])
        tile = tile_of(sums)
        for k in range(tiles.shape[0]):
            for piece in range(group):
                tiles[k, pl.ds(piece, rows // 2, stride=group), :] = up[
                    piece * rows // 2:(piece + 1) * rows // 2, k * lanes:(k + 1) * lanes
                ]
            spread_down[k * lanes:(k + 1) * lanes, :] = tiles[k].T
        for b in range(blocks):
            for h in range(2):
                at = (2 * b + h) * half
                p_ref[b, h, 0:half] = spread_down[at:at + half, :]
                p_ref[b, h, half:] = jnp.zeros((p_ref.shape[2] - half, lanes), jnp.float32)
            p_ref[b, 0, half:half + 8] = tile
        exchange(blocks, p_ref, *links)
        for b in range(blocks):
            out_ref[b] = links[0][b]


def coeff_call(kind, cycle_count, lanes, *operands):
    legendre_at = 2
    slots, degrees, cycles = operands[legendre_at].shape
    rows = lanes // slots
    blocks, _, padded, _ = operands[0].shape
    in_specs = []
    for place, operand in enumerate(operands):
        if place >= legendre_at and operand.ndim == 3:
            in_specs.append(pl.BlockSpec((1,) + operand.shape[1:], lambda s: (s, 0, 0)))
        elif place >= legendre_at and operand.ndim == 4:
            in_specs.append(pl.BlockSpec((1,) + operand.shape[1:], lambda s: (s, 0, 0, 0)))
        elif operand.ndim == 1:
            in_specs.append(pl.BlockSpec(memory_space=pltpu.SMEM))
        else:
            in_specs.append(VMEM_WHOLE)
    vector = jax.ShapeDtypeStruct((slots, rows, degrees), jnp.float32)
    vector_spec = pl.BlockSpec((1, rows, degrees), lambda s: (s, 0, 0))
    partial = jax.ShapeDtypeStruct(operands[0].shape, jnp.float32)
    scratch = [
        pltpu.VMEM((cycles, lanes), jnp.float32),
        pltpu.VMEM((lanes, cycles), jnp.float32),
        pltpu.VMEM((cycles // lanes, lanes, lanes), jnp.float32),
    ]
    if kind == "last":
        out_shape, out_specs = [vector] * 2, [vector_spec] * 2
    else:
        vectors = 2 if kind == "first" else 3
        out_shape = [partial] + [vector] * vectors
        out_specs = [VMEM_WHOLE] + [vector_spec] * vectors
        if kind == "first":
            for shape in ((degrees, cycles), (degrees, degrees)):
                out_shape += [jax.ShapeDtypeStruct((slots,) + shape, jnp.bfloat16)] * 2
                out_specs += [pl.BlockSpec((1,) + shape, lambda s: (s, 0, 0))] * 2
        scratch.append(pltpu.VMEM((lanes, cycles), jnp.float32))
        scratch.append(pltpu.VMEM((3, lanes, lanes), jnp.float32))
    if kind != "first":
        scratch.append(pltpu.VMEM((2, rows, lanes), jnp.float32))
    params = {"vmem_limit_bytes": 60 << 20}
    if kind != "last":
        scratch += exchange_scratch(blocks, padded, lanes)
        params.update(collective_id=3 if kind == "first" else 4, has_side_effects=True)
    return pl.pallas_call(
        functools.partial(coeff_kernel, kind, cycle_count // 2),
        grid=(slots,),
        out_shape=out_shape,
        in_specs=in_specs,
        out_specs=out_specs,
        scratch_shapes=scratch,
        compiler_params=pltpu.CompilerParams(**params),
        name="coeff_" + kind,
    )(*operands)


def fast_body(anomalies, classes, legendre, precond, prior, assign):
    lon_count = lax.axis_size("lon")
    blocks = lax.axis_size("blk")
    blk_place = lax.axis_index("blk")
    lon_place = lax.axis_index("lon")
    slot_count, local_degrees, _ = legendre.shape
    rhs_count, cycle_count, longitudes = anomalies.shape
    window = assign.shape[0]
    block_width = precond.shape[2]
    lanes = slot_count * 2 * rhs_count
    stride_value = local_degrees * lon_count // window
    all_orders = assign * stride_value
    own_orders = lax.dynamic_slice_in_dim(all_orders, blk_place * slot_count, slot_count)
    places = jnp.concatenate([own_orders, (lon_place * local_degrees)[None]])
    pair_orders = jnp.repeat(all_orders, 2)[:, None]
    column = lon_place * longitudes + jnp.arange(longitudes, dtype=jnp.int32)
    phases = pair_orders * column[None, :] % (longitudes * lon_count)
    angles = phases.astype(jnp.float32) * (2.0 * math.pi / (longitudes * lon_count))
    sine = (jnp.arange(2 * window) % 2 == 1)[:, None]
    trig = jnp.where(sine, jnp.sin(angles), jnp.cos(angles))
    prior_row = prior[None, :]

    sizes = (blocks, lanes, cycle_count, rhs_count)
    sums, *tables = grid_call("data", *sizes, anomalies, classes, trig)
    first_up, residual, direction, *factors = coeff_call(
        "first", cycle_count, lanes, sums, places, legendre, precond, prior_row
    )
    sums, scalars = grid_call("first", *sizes, first_up, *tables)
    second_up, residual, search, solved = coeff_call(
        "middle", cycle_count, lanes, sums, scalars, *factors, places, prior_row,
        residual, direction,
    )
    sums, scalars = grid_call("next", *sizes, second_up, first_up, scalars, *tables)
    residual, solved = coeff_call(
        "last", cycle_count, lanes, sums, scalars, *factors[:2], places, prior_row,
        residual, direction, search, solved,
    )
    shape = (slot_count, 2, rhs_count, local_degrees)
    return solved.reshape(shape), residual.reshape(shape)


def body(anomalies, classes, legendre, precond, prior, assign):
    fits = (
        lax.axis_size("lon") == 4
        and lax.axis_size("blk") % 2 == 0
        and anomalies.shape[1] % 16 == 0
        and legendre.shape[0] * 2 == GROUP
        and legendre.shape[2] % 128 == 0
        and legendre.shape[0] * 2 * anomalies.shape[0] == 128
    )
    chosen = fast_body if fits else plain_body
    return chosen(anomalies, classes, legendre, precond, prior, assign)


def solution(mesh):
    in_specs = (
        P(None, "blk", "lon"),
        P("blk", "lon"),
        P("blk", "lon", None),
        P("blk", "lon", None, None),
        P("lon"),
        P(),
    )
    out_specs = (P("blk", None, None, "lon"), P("blk", None, None, "lon"))
    return jax.shard_map(body, mesh=mesh, in_specs=in_specs, out_specs=out_specs, check_vma=False)
```

```python
import functools
import math

import jax
import jax.numpy as jnp
from jax import lax
from jax.experimental import pallas as pl
from jax.experimental.pallas import tpu as pltpu
from jax.sharding import PartitionSpec as P

ITERS = 2


HUBER_LEVELS = (1.0, 0.5, 0.25, 0.125)
HIGHEST = lax.Precision.HIGHEST
GROUP = 8
NEVER = 2**30
MESH = pl.DeviceIdType.MESH
VMEM_WHOLE = pl.BlockSpec(memory_space=pltpu.VMEM)


def build_mask(orders, first_degree, degrees):
    degree = first_degree + jnp.arange(degrees, dtype=jnp.int32)
    upper_part = (degree[None, :] >= orders[:, None]).astype(jnp.float32)
    sine_keep = upper_part * (orders[:, None] > 0).astype(jnp.float32)
    return jnp.stack([upper_part, sine_keep], axis=1)[:, :, None, :]


def trig_table(orders, first_col, columns, lon_total):
    column = first_col + jnp.arange(columns, dtype=jnp.int32)
    phases = orders[:, None] * column[None, :] % lon_total
    angles = phases.astype(jnp.float32) * (2.0 * math.pi / lon_total)
    return jnp.stack([jnp.cos(angles), jnp.sin(angles)], axis=1)


def huber_weights(classes):
    weighted = jnp.zeros(classes.shape, jnp.float32)
    for level_index in range(4):
        weighted = (
            weighted + (classes == level_index).astype(jnp.float32) * HUBER_LEVELS[level_index]
        )
    return weighted


def legendre_up(coeffs, basis_rows):
    return jnp.einsum("scnl,slr->scnr", coeffs, basis_rows, precision=HIGHEST)


def legendre_down(cycles_part, basis_rows):
    return jnp.einsum("scnr,slr->scnl", cycles_part, basis_rows, precision=HIGHEST)


def plain_body(anomalies, classes, legendre, precond, prior, assign):
    lon_count = lax.axis_size("lon")
    blk_count = lax.axis_size("blk")
    blk_place = lax.axis_index("blk")
    lon_place = lax.axis_index("lon")
    slot_count = legendre.shape[0]
    local_degrees = legendre.shape[1]
    rhs_count = anomalies.shape[0]
    cycle_count = anomalies.shape[1]
    longitudes = anomalies.shape[2]
    window = assign.shape[0]
    block_width = precond.shape[2]
    quarter = slot_count // lon_count
    grid_rows = rhs_count * cycle_count
    stride_value = local_degrees * lon_count // window
    all_orders = assign * stride_value
    own_orders = lax.dynamic_slice_in_dim(all_orders, blk_place * slot_count, slot_count)
    first_degree = lon_place * local_degrees
    first_column = lon_place * longitudes
    live_mask = build_mask(own_orders, first_degree, local_degrees)
    weights = huber_weights(classes)
    row_orders = (
        all_orders.reshape(blk_count, lon_count, quarter).transpose(1, 0, 2).reshape(window)
    )
    trig_rows = trig_table(row_orders, first_column, longitudes, longitudes * lon_count).reshape(
        2 * window, longitudes
    )

    def analyse(grid_field):
        flat_grid = grid_field.reshape(grid_rows, longitudes)
        product = lax.dot_general(trig_rows, flat_grid, (((1,), (1,)), ((), ())), precision=HIGHEST)
        shared = lax.psum_scatter(
            product.reshape(window // lon_count * lax.axis_size("lon"), 2, rhs_count, cycle_count),
            "lon",
            scatter_dimension=0,
            tiled=True,
        )
        returned = lax.all_to_all(shared, "blk", split_axis=0, concat_axis=3, tiled=True)
        return legendre_down(lax.all_gather(returned, "lon", axis=0, tiled=True), legendre)

    def precondition(coeffs):
        blocks = coeffs.reshape(slot_count, 2, rhs_count, local_degrees // block_width, block_width)
        applied = jnp.einsum("sbij,scnbj->scnbi", precond, blocks, precision=HIGHEST)
        return live_mask * applied.reshape(coeffs.shape)

    def column_dot(lhs_values, rhs_values):
        return jnp.sum(lhs_values * rhs_values, axis=(0, 1, 3))

    def spread(values):
        return values[None, None, :, None]

    def fit_sum(lhs_values, rhs_values):
        return lax.psum(column_dot(lhs_values, rhs_values), ("blk", "lon"))

    residual = live_mask * analyse(weights * anomalies)
    solution = jnp.zeros_like(residual)
    search = precondition(residual)
    fit_now = fit_sum(residual, search)
    direction = search
    for iteration in range(ITERS):
        synthesize_coeffs = direction
        synthesize_shared = lax.psum_scatter(
            legendre_up(synthesize_coeffs, legendre), "lon", scatter_dimension=0, tiled=True
        )
        moved = lax.all_to_all(synthesize_shared, "blk", split_axis=3, concat_axis=0, tiled=True)
        flat_orders = lax.all_gather(moved, "lon", axis=0, tiled=True).reshape(-1, grid_rows)
        grid_flat = lax.dot_general(
            flat_orders, trig_rows, (((0,), (0,)), ((), ())), precision=HIGHEST
        )
        image_vec = live_mask * (
            analyse(weights * grid_flat.reshape(rhs_count, cycle_count, longitudes))
            + prior * direction
        )
        curvature_sum = lax.psum(column_dot(direction, image_vec), ("blk", "lon"))
        alpha_step = fit_now / curvature_sum
        solution = solution + spread(alpha_step) * direction
        residual = residual - spread(alpha_step) * image_vec
        if iteration + 1 < ITERS:
            search = precondition(residual)
            fit_next = fit_sum(residual, search)
            direction = search + spread(fit_next / fit_now) * direction
            fit_now = fit_next
    return (solution, residual)


def split(values):
    high = values.astype(jnp.bfloat16)
    return high, (values - high.astype(jnp.float32)).astype(jnp.bfloat16)


def mates():
    blk = lax.axis_index("blk")
    lon = lax.axis_index("lon")
    core, x = lon % 2, lon // 2
    return blk, lon, core, x, (blk, lon + 1 - 2 * core), (blk, lon + 2 - 4 * x)


def greet(blocks):
    blk, lon, _, _, core_mate, x_mate = mates()
    barrier = pltpu.get_barrier_semaphore()
    peers = [core_mate, x_mate] + [((blk + j) % blocks, lon) for j in range(1, blocks)]
    for peer in peers:
        pl.semaphore_signal(barrier, inc=1, device_id=peer, device_id_type=MESH)


def exchange(blocks, p_ref, landed, from_core, summed, from_x, ready, send_sem, recv_sem,
             between=lambda: None):
    blk, lon, core, x, core_mate, x_mate = mates()
    o_ref = landed
    pl.semaphore_wait(pltpu.get_barrier_semaphore(), blocks + 1)
    part = from_x.shape[1]
    mine = pl.ds(pl.multiple_of(part * x, 8), part)
    theirs = pl.ds(pl.multiple_of(part * (1 - x), 8), part)

    def copy(stage, j, src, dst, peer):
        return pltpu.make_async_remote_copy(
            src_ref=src,
            dst_ref=dst,
            send_sem=send_sem.at[stage, j],
            recv_sem=recv_sem.at[stage, j],
            device_id=peer,
            device_id_type=MESH,
        )

    order = sorted(range(blocks), key=lambda j: (j == 0, abs(j - blocks // 2)))
    started = {}

    def launch(stage, j, src, dst, peer):
        started[stage, j] = copy(stage, j, src, dst, peer)
        started[stage, j].start()

    for j in order:
        to = (blk + j) % blocks
        launch(0, j, p_ref.at[to, 1 - core], from_core.at[to], core_mate)

    def over_x(j):
        to = (blk + j) % blocks
        started[0, j].wait_recv()
        summed[to] = p_ref[to, core] + from_core[to]
        launch(1, j, summed.at[to, theirs], from_x.at[to], x_mate)

    def over_blk(j):
        to = (blk + j) % blocks
        started[1, j].wait_recv()
        value = summed[to, mine] + from_x[to]
        if j == 0:
            o_ref[blk, core, mine] = value
        else:
            ready[to] = value
            launch(2, j, ready.at[to], o_ref.at[blk, core, mine], (to, lon))

    for j in order:
        over_x(j)
    for j in order:
        over_blk(j)
    between()
    arrivals = order[-1:] + order[:-1]
    for j in arrivals:
        source = (blk - j + blocks) % blocks
        if j:
            started[2, j].wait_recv()
        held = o_ref.at[source, core, mine]
        launch(3, j, held, held, x_mate)
        launch(4, j, held, held, core_mate)
    for j in arrivals:
        source = (blk - j + blocks) % blocks
        started[3, j].wait_recv()
        held = o_ref.at[source, core, theirs]
        launch(5, j, held, held, core_mate)
    for j in arrivals:
        started[4, j].wait_recv()
        started[5, j].wait_recv()
    for one in started.values():
        one.wait_send()


def exchange_scratch(blocks, padded, lanes):
    return [
        pltpu.VMEM((blocks, 2, padded, lanes), jnp.float32),
        pltpu.VMEM((blocks, 2, padded, lanes), jnp.float32),
        pltpu.VMEM((blocks, padded, lanes), jnp.float32),
        pltpu.VMEM((blocks, padded, lanes), jnp.float32),
        pltpu.VMEM((blocks, padded // 2, lanes), jnp.float32),
        pltpu.VMEM((blocks, padded // 2, lanes), jnp.float32),
        pltpu.SemaphoreType.DMA((6, blocks)),
        pltpu.SemaphoreType.DMA((6, blocks)),
    ]


def group_sum(tile, group):
    lanes = tile.shape[1]
    at = lax.broadcasted_iota(jnp.int32, tile.shape, 1)
    shift = 1
    while shift < group:
        ahead = pltpu.roll(tile, lanes - shift, 1)
        behind = pltpu.roll(tile, shift, 1)
        tile = tile + jnp.where(at // shift % 2 == 0, ahead, behind)
        shift *= 2
    return tile


def sums_of(o_ref, half, group):
    tile = o_ref[0, 0, half:half + 8]
    for b in range(1, o_ref.shape[0]):
        tile = tile + o_ref[b, 0, half:half + 8]
    return group_sum(tile, group)


def pick_row(tile, row):
    return tile[row:row + 1]


def tile_of(rows):
    lanes = rows[0].shape[1]
    at = lax.broadcasted_iota(jnp.int32, (8, lanes), 0)
    tile = jnp.zeros((8, lanes), jnp.float32)
    for index, row in enumerate(rows):
        tile = jnp.where(at == index, jnp.broadcast_to(row, (8, lanes)), tile)
    return tile


def grid_kernel(kind, half, batch, *refs):
    steps = pl.num_programs(0)
    step = pl.program_id(0)
    refs, p_ref, links = refs[:-8], refs[-8], refs[-7:]
    if kind == "data":
        (field, classes, trig, turned_leg, out_ref, weights, trig_up, trig_down, trig_low, leg_out,
         down, leg_buffer, leg_sem) = refs
    elif kind == "first":
        o_ref, weights, trig_up, trig_down, trig_low, out_ref, q_ref, down, up, cycles = refs
    else:
        (o_ref, old_ref, old_q, weights, trig_up, trig_down, trig_low,
         out_ref, q_ref, down, up, cycles) = refs
    blocks, lanes = down.shape[0], down.shape[1]
    group = GROUP
    cycle_count = 2 * half

    @pl.when(step == 0)
    def _():
        greet(blocks)

    if kind == "data":
        def fetch(slot):
            return pltpu.make_async_copy(
                turned_leg.at[:, slot, :], leg_buffer.at[slot], leg_sem.at[0, slot]
            )

        def store(slot):
            return pltpu.make_async_copy(
                leg_buffer.at[slot], leg_out.at[slot], leg_sem.at[1, slot]
            )

        slots = range(leg_buffer.shape[0])

        @pl.when(step == 0)
        def _():
            for slot in slots:
                fetch(slot).start()
            level = classes[...]
            weighted = jnp.zeros(level.shape, jnp.float32)
            for index, value in enumerate(HUBER_LEVELS):
                weighted = jnp.where(level == index, value, weighted)
            weights[...] = weighted
            table = trig[...]
            high = table.astype(jnp.bfloat16).astype(jnp.float32)
            rest = table - high
            trig_up[...] = jnp.concatenate([high, rest, high], axis=0).astype(jnp.bfloat16)
            trig_down[...] = jnp.concatenate([high, rest], axis=0).T.astype(jnp.bfloat16)
            trig_low[...] = (
                jnp.concatenate([high, jnp.zeros_like(high)], axis=0).T.astype(jnp.bfloat16)
            )
    else:
        @pl.when(step == 0)
        def _():
            sums = sums_of(o_ref, half, group)
            if kind == "first":
                q_ref[...] = sums
            else:
                before = old_q[...]
                beta = pick_row(sums, 0) / pick_row(before, 0)
                norm = (
                    pick_row(sums, 1)
                    + 2.0 * beta * pick_row(sums, 2)
                    + beta * beta * pick_row(before, 1)
                )
                q_ref[...] = tile_of([pick_row(sums, 0), norm, beta])
            for b in range(blocks):
                for h in range(2):
                    rows = o_ref[b, h, 0:half]
                    if kind != "first":
                        rows = rows + beta * old_ref[b, h, 0:half]
                    cycles[b, h * half:(h + 1) * half] = rows
                up[b] = cycles[b].T

    def place(inner):
        return pl.ds(pl.multiple_of((step * batch + inner) * group, 8), group)

    if kind == "data":
        grids = [field[inner] for inner in range(batch)]
    else:
        triples = []
        for inner in range(batch):
            stack = jnp.concatenate(
                [up[b, place(inner), :] for b in range(blocks)], axis=0
            )
            high = stack.astype(jnp.bfloat16).astype(jnp.float32)
            triple = jnp.concatenate([high, high, stack - high], axis=0)
            triples.append(triple.T.astype(jnp.bfloat16))
        fields = jnp.dot(
            jnp.concatenate(triples, axis=0), trig_up[...], preferred_element_type=jnp.float32
        )
        grids = [
            fields[inner * cycle_count:(inner + 1) * cycle_count] for inner in range(batch)
        ]
    scale = weights[...]
    parts = [split(one * scale) for one in grids]
    high = jnp.concatenate([part[0] for part in parts], axis=0)
    low = jnp.concatenate([part[1] for part in parts], axis=0)
    sums = jnp.dot(high, trig_down[...], preferred_element_type=jnp.float32)
    sums = sums + jnp.dot(low, trig_low[...], preferred_element_type=jnp.float32)
    for inner in range(batch):
        turned = sums[inner * cycle_count:(inner + 1) * cycle_count].T
        turned = turned[: group * blocks] + turned[group * blocks:]
        for b in range(blocks):
            down[b, place(inner), :] = turned[group * b:group * (b + 1)]

    @pl.when(step == steps - 1)
    def _():
        total = jnp.zeros((1, lanes), jnp.float32)
        for b in range(blocks):
            rows = down[b].T
            if kind != "data":
                total = total + jnp.sum(rows * cycles[b], axis=0, keepdims=True)
            for h in range(2):
                p_ref[b, h, 0:half] = rows[h * half:(h + 1) * half]
        for b in range(blocks):
            for h in range(2):
                p_ref[b, h, half:] = jnp.zeros((p_ref.shape[2] - half, lanes), jnp.float32)
            if kind != "data":
                p_ref[b, 0, half:half + 8] = tile_of([total])
        def relay():
            if kind == "data":
                for slot in slots:
                    fetch(slot).wait()
                    store(slot).start()

        exchange(blocks, p_ref, *links, between=relay)
        for b in range(blocks):
            out_ref[b] = links[0][b]
        if kind == "data":
            for slot in slots:
                store(slot).wait()


def grid_call(kind, blocks, lanes, cycle_count, rhs_count, *operands):
    half = cycle_count // 2
    padded = -(-(half + 8) // 16) * 16
    batch = 4 if rhs_count % 4 == 0 else 1
    out_shape = [jax.ShapeDtypeStruct((blocks, 2, padded, lanes), jnp.float32)]
    scratch = [pltpu.VMEM((blocks, lanes, cycle_count), jnp.float32)]
    in_specs = [VMEM_WHOLE] * len(operands)
    if kind == "data":
        shape = operands[0].shape
        in_specs[0] = pl.BlockSpec((batch,) + shape[1:], lambda n: (n, 0, 0))
        rows = operands[2].shape[0]
        degrees, slots, cycles = operands[3].shape
        in_specs[3] = pl.BlockSpec(memory_space=pl.ANY)
        out_shape += [
            jax.ShapeDtypeStruct(shape[1:], jnp.float32),
            jax.ShapeDtypeStruct((3 * rows, shape[2]), jnp.bfloat16),
            jax.ShapeDtypeStruct((shape[2], 2 * rows), jnp.bfloat16),
            jax.ShapeDtypeStruct((shape[2], 2 * rows), jnp.bfloat16),
            jax.ShapeDtypeStruct((slots, degrees, cycles), jnp.float32),
        ]
        scratch.append(pltpu.VMEM((slots, degrees, cycles), jnp.float32))
        scratch.append(pltpu.SemaphoreType.DMA((2, slots)))
    else:
        out_shape.append(jax.ShapeDtypeStruct((8, lanes), jnp.float32))
        scratch.append(pltpu.VMEM((blocks, lanes, cycle_count), jnp.float32))
        scratch.append(pltpu.VMEM((blocks, cycle_count, lanes), jnp.float32))
    scratch += exchange_scratch(blocks, padded, lanes)
    out_specs = [VMEM_WHOLE] * len(out_shape)
    if kind == "data":
        out_specs[-1] = pl.BlockSpec(memory_space=pl.ANY)
    return pl.pallas_call(
        functools.partial(grid_kernel, kind, half, batch),
        grid=(rhs_count // batch,),
        out_shape=out_shape,
        in_specs=in_specs,
        out_specs=out_specs,
        scratch_shapes=scratch,
        compiler_params=pltpu.CompilerParams(
            vmem_limit_bytes=60 << 20,
            collective_id=("data", "first", "next").index(kind),
            has_side_effects=True,
        ),
        name="grid_" + kind,
    )(*operands)


def to_column(row):
    return jnp.broadcast_to(row, (row.shape[1], row.shape[1])).T


def product(lhs, high, low, dims):
    lhs_high, lhs_low = split(lhs)
    rows = lhs.shape[0]
    both = jnp.concatenate([lhs_high, lhs_low], axis=0)
    first = lax.dot_general(both, high, dims, preferred_element_type=jnp.float32)
    second = lax.dot_general(lhs_high, low, dims, preferred_element_type=jnp.float32)
    return first[:rows] + first[rows:] + second


NN = (((1,), (0,)), ((), ()))
NT = (((1,), (1,)), ((), ()))


def block_diagonal(blocks_ref):
    _, count, width, _ = blocks_ref.shape
    rows = []
    for index in range(count):
        parts = []
        if index:
            parts.append(jnp.zeros((width, width * index), jnp.float32))
        parts.append(blocks_ref[0, index])
        if index + 1 < count:
            parts.append(jnp.zeros((width, width * (count - 1 - index)), jnp.float32))
        rows.append(jnp.concatenate(parts, axis=1))
    return jnp.concatenate(rows, axis=0)


def coeff_kernel(kind, half, *refs):
    s = pl.program_id(0)
    if kind != "last":
        refs, p_ref, links = refs[:-8], refs[-8], refs[-7:]
    if kind == "first":
        (o_ref, places, legendre, precond, prior,
         out_ref, residual, z_out, leg_high, leg_low, pre_high, pre_low,
         spread_down, turned_down, tiles, up, dots) = refs
    elif kind == "middle":
        (o_ref, q_ref, leg_high, leg_low, pre_high, pre_low, places, prior, old, direction,
         out_ref, residual, z_out, solution, spread_down, turned_down, tiles, up, dots, alphas) = refs
    else:
        (o_ref, q_ref, leg_high, leg_low, places, prior, old, direction, z_in, old_solution,
         residual, solution, spread_down, turned_down, tiles, alphas) = refs
    blocks = o_ref.shape[0]
    lanes = o_ref.shape[3]
    group = GROUP
    rows = residual.shape[1]

    @pl.when(s == 0)
    def _():
        if kind != "last":
            greet(blocks)
        for b in range(blocks):
            for h in range(2):
                spread_down[(2 * b + h) * half:(2 * b + h + 1) * half, :] = o_ref[b, h, 0:half]
        for k in range(tiles.shape[0]):
            tiles[k] = spread_down[k * lanes:(k + 1) * lanes, :].T
            for piece in range(group):
                turned_down[piece * rows // 2:(piece + 1) * rows // 2, k * lanes:(k + 1) * lanes] = tiles[
                    k, pl.ds(piece, rows // 2, stride=group), :
                ]
        if kind != "first":
            sums = sums_of(o_ref, half, group)
            scalars = q_ref[...]
            alpha = pick_row(scalars, 0) / (pick_row(sums, 0) + pick_row(scalars, 1))
            wanted = [alpha, pick_row(scalars, 2)] if kind == "last" else [alpha]
            for index, row in enumerate(wanted):
                tiles[0] = to_column(row)
                once = tiles[0, pl.ds(0, rows // 2, stride=group), :]
                alphas[index] = jnp.concatenate([once, once], axis=0)

    where = pl.ds(pl.multiple_of(s * rows, rows), rows)
    if kind == "first":
        leg_high[0], leg_low[0] = split(legendre[0])
        pre_high[0], pre_low[0] = split(block_diagonal(precond))
    cycles = turned_down[where, :]
    image = product(cycles, leg_high[0], leg_low[0], NT)
    order = places[s]
    degree = places[pl.num_programs(0)] + lax.broadcasted_iota(jnp.int32, residual.shape[1:], 1)
    sine = lax.broadcasted_iota(jnp.int32, residual.shape[1:], 0) >= rows // 2
    least = jnp.where(sine, jnp.maximum(order, jnp.where(order == 0, NEVER, 0)), order)
    mask = (degree >= least).astype(jnp.float32)
    if kind == "first":
        res = mask * image
    else:
        alpha = alphas[0, :, 0:1]
        d = direction[0]
        if kind == "last":
            d = z_in[0] + alphas[1, :, 0:1] * d
        image = mask * (image + prior[...] * d)
        res = old[0] - alpha * image
        if kind == "last":
            solution[0] = old_solution[0] + alpha * d
        else:
            solution[0] = alpha * d
    residual[0] = res
    if kind == "last":
        return
    z = mask * product(res, pre_high[0], pre_low[0], NN)
    z_out[0] = z
    pairs = [res * z, prior[...] * z * z]
    if kind == "middle":
        pairs.append(prior[...] * z * d)
    for index, pair in enumerate(pairs):
        dots[index, where, :] = jnp.broadcast_to(
            jnp.sum(pair, axis=1, keepdims=True), (rows, lanes)
        )
    up[where, :] = product(z, leg_high[0], leg_low[0], NN)

    @pl.when(s == pl.num_programs(0) - 1)
    def _():
        sums = []
        for index in range(len(pairs)):
            column = dots[index, 0:rows // 2]
            for piece in range(1, group):
                column = column + dots[index, piece * rows // 2:(piece + 1) * rows // 2]
            tiles[0] = jnp.zeros((lanes, lanes), jnp.float32)
            tiles[0, pl.ds(0, rows // 2, stride=group), :] = column
            sums.append(tiles[0].T[0:1])
        tile = tile_of(sums)
        for k in range(tiles.shape[0]):
            for piece in range(group):
                tiles[k, pl.ds(piece, rows // 2, stride=group), :] = up[
                    piece * rows // 2:(piece + 1) * rows // 2, k * lanes:(k + 1) * lanes
                ]
            spread_down[k * lanes:(k + 1) * lanes, :] = tiles[k].T
        for b in range(blocks):
            for h in range(2):
                at = (2 * b + h) * half
                p_ref[b, h, 0:half] = spread_down[at:at + half, :]
                p_ref[b, h, half:] = jnp.zeros((p_ref.shape[2] - half, lanes), jnp.float32)
            p_ref[b, 0, half:half + 8] = tile
        exchange(blocks, p_ref, *links)
        for b in range(blocks):
            out_ref[b] = links[0][b]


def coeff_call(kind, cycle_count, lanes, *operands):
    legendre_at = 2
    slots, degrees, cycles = operands[legendre_at].shape
    rows = lanes // slots
    blocks, _, padded, _ = operands[0].shape
    in_specs = []
    for place, operand in enumerate(operands):
        if place >= legendre_at and operand.ndim == 3:
            in_specs.append(pl.BlockSpec((1,) + operand.shape[1:], lambda s: (s, 0, 0)))
        elif place >= legendre_at and operand.ndim == 4:
            in_specs.append(pl.BlockSpec((1,) + operand.shape[1:], lambda s: (s, 0, 0, 0)))
        elif operand.ndim == 1:
            in_specs.append(pl.BlockSpec(memory_space=pltpu.SMEM))
        else:
            in_specs.append(VMEM_WHOLE)
    vector = jax.ShapeDtypeStruct((slots, rows, degrees), jnp.float32)
    vector_spec = pl.BlockSpec((1, rows, degrees), lambda s: (s, 0, 0))
    partial = jax.ShapeDtypeStruct(operands[0].shape, jnp.float32)
    scratch = [
        pltpu.VMEM((cycles, lanes), jnp.float32),
        pltpu.VMEM((lanes, cycles), jnp.float32),
        pltpu.VMEM((cycles // lanes, lanes, lanes), jnp.float32),
    ]
    if kind == "last":
        out_shape, out_specs = [vector] * 2, [vector_spec] * 2
    else:
        vectors = 2 if kind == "first" else 3
        out_shape = [partial] + [vector] * vectors
        out_specs = [VMEM_WHOLE] + [vector_spec] * vectors
        if kind == "first":
            for shape in ((degrees, cycles), (degrees, degrees)):
                out_shape += [jax.ShapeDtypeStruct((slots,) + shape, jnp.bfloat16)] * 2
                out_specs += [pl.BlockSpec((1,) + shape, lambda s: (s, 0, 0))] * 2
        scratch.append(pltpu.VMEM((lanes, cycles), jnp.float32))
        scratch.append(pltpu.VMEM((3, lanes, lanes), jnp.float32))
    if kind != "first":
        scratch.append(pltpu.VMEM((2, rows, lanes), jnp.float32))
    params = {"vmem_limit_bytes": 60 << 20}
    if kind != "last":
        scratch += exchange_scratch(blocks, padded, lanes)
        params.update(collective_id=3 if kind == "first" else 4, has_side_effects=True)
    return pl.pallas_call(
        functools.partial(coeff_kernel, kind, cycle_count // 2),
        grid=(slots,),
        out_shape=out_shape,
        in_specs=in_specs,
        out_specs=out_specs,
        scratch_shapes=scratch,
        compiler_params=pltpu.CompilerParams(**params),
        name="coeff_" + kind,
    )(*operands)


def fast_body(anomalies, classes, legendre, precond, prior, assign):
    lon_count = lax.axis_size("lon")
    blocks = lax.axis_size("blk")
    blk_place = lax.axis_index("blk")
    lon_place = lax.axis_index("lon")
    slot_count, local_degrees, _ = legendre.shape
    rhs_count, cycle_count, longitudes = anomalies.shape
    window = assign.shape[0]
    block_width = precond.shape[2]
    lanes = slot_count * 2 * rhs_count
    stride_value = local_degrees * lon_count // window
    all_orders = assign * stride_value
    own_orders = lax.dynamic_slice_in_dim(all_orders, blk_place * slot_count, slot_count)
    places = jnp.concatenate([own_orders, (lon_place * local_degrees)[None]])
    pair_orders = jnp.repeat(all_orders, 2)[:, None]
    column = lon_place * longitudes + jnp.arange(longitudes, dtype=jnp.int32)
    phases = pair_orders * column[None, :] % (longitudes * lon_count)
    angles = phases.astype(jnp.float32) * (2.0 * math.pi / (longitudes * lon_count))
    sine = (jnp.arange(2 * window) % 2 == 1)[:, None]
    trig = jnp.where(sine, jnp.sin(angles), jnp.cos(angles))
    prior_row = prior[None, :]

    sizes = (blocks, lanes, cycle_count, rhs_count)
    sums, *tables, ordered = grid_call(
        "data", *sizes, anomalies, classes, trig, legendre.transpose(1, 0, 2)
    )
    first_up, residual, direction, *factors = coeff_call(
        "first", cycle_count, lanes, sums, places, ordered, precond, prior_row
    )
    sums, scalars = grid_call("first", *sizes, first_up, *tables)
    second_up, residual, search, solved = coeff_call(
        "middle", cycle_count, lanes, sums, scalars, *factors, places, prior_row,
        residual, direction,
    )
    sums, scalars = grid_call("next", *sizes, second_up, first_up, scalars, *tables)
    residual, solved = coeff_call(
        "last", cycle_count, lanes, sums, scalars, *factors[:2], places, prior_row,
        residual, direction, search, solved,
    )
    shape = (slot_count, 2, rhs_count, local_degrees)
    return solved.reshape(shape), residual.reshape(shape)


def body(anomalies, classes, legendre, precond, prior, assign):
    fits = (
        lax.axis_size("lon") == 4
        and lax.axis_size("blk") % 2 == 0
        and anomalies.shape[1] % 16 == 0
        and legendre.shape[0] * 2 == GROUP
        and legendre.shape[2] % 128 == 0
        and legendre.shape[0] * 2 * anomalies.shape[0] == 128
    )
    chosen = fast_body if fits else plain_body
    return chosen(anomalies, classes, legendre, precond, prior, assign)


def solution(mesh):
    in_specs = (
        P(None, "blk", "lon"),
        P("blk", "lon"),
        P("blk", "lon", None),
        P("blk", "lon", None, None),
        P("lon"),
        P(),
    )
    out_specs = (P("blk", None, None, "lon"), P("blk", None, None, "lon"))
    return jax.shard_map(body, mesh=mesh, in_specs=in_specs, out_specs=out_specs, check_vma=False)
```
